256 devices in a mesh: dp: 4 (over y_lo, core), tile: 64 (over y_hi, x, z).
Axes of the slice: x: 4, y: 4 (y_hi: 2, y_lo: 2; y = y_hi * 2 + y_lo), z: 8, core: 2. Of those that a mesh axis runs over, the one named last changes fastest.
Arguments:
- inputs: bfloat16 [8, 64, 1024, 256], P('dp', None, 'tile'), may hold values from -6 to 6
- cotangent: bfloat16 [8, 64, 1024, 256], P('dp', None, 'tile'), may hold values from -6 to 6
- mode_weight: bfloat16 [64, 64, 64, 128], P('tile'), may hold values from -0.5 to 0.5
- local_weight: bfloat16 [64, 64], replicated, may hold values from -0.75 to 0.75
Outputs:
- input_grad: bfloat16 [8, 64, 1024, 256], P('dp', None, 'tile')
- mode_grad: float32 [64, 64, 64, 128], P('tile')
- local_grad: float32 [64, 64], replicated
The draws below stay inside these ranges and needn't reach their ends.
All inputs are finite; a program needn't handle non-finite values.
Results may differ from the reference program's by a relative error of at most 0.015.
Values may be sent and summed in bfloat16 or wider, within the bound.
A program may use at most 64 MiB of HBM per device.

```python
import math
import jax
import jax.numpy as jnp
from jax import lax

C = 64
M1 = 64
M2 = 64
W = 256
TH = 16
H = 1024
SAMPLES = 8
N_TILE = 64


def shard_levels(key, extent, split, least, top_value):
    factor_of = 1.0
    for position, parts in split:
        draws = jax.random.uniform(jax.random.fold_in(jax.random.fold_in(key, 6), position), (parts,), jnp.float32, least / len(split), top_value / len(split))
        factor_of = factor_of * jnp.repeat(jnp.exp(draws), extent[position] // parts).reshape((-1,) + (1,) * (len(extent) - 1 - position))
    return factor_of


def normal_values(rng, extent, scale, reach, shards=(), kind=jnp.bfloat16):
    gain = shard_levels(rng, extent, shards, -0.22, 0.18) if shards else 1.0
    drawn = jax.random.normal(rng, extent, jnp.float32) * scale * gain
    return jnp.minimum(jnp.maximum(drawn, -reach), reach).astype(kind)


def setup_inputs(seed: int = 0) -> dict:
    keys = jax.random.split(jax.random.key(seed), 5)
    inputs = normal_values(keys[0], (SAMPLES, C, H, W), 1.0, 6.0, ((0, 4), (2, 64)))
    cotangent = normal_values(keys[1], (SAMPLES, C, H, W), 1.0, 6.0, ((0, 4), (2, 64)))
    mode_weight = normal_values(keys[2], (M2, C, C, 2 * M1), (2 * C) ** -0.5, 0.5, ((0, 64),))
    local_weight = normal_values(keys[3], (C, C), C ** -0.5, 0.75)
    return {"inputs": inputs, "cotangent": cotangent, "mode_weight": mode_weight, "local_weight": local_weight}


def row_tables(positions, length):
    modes = jnp.arange(M1, dtype=jnp.int32)
    signed = jnp.where(modes < M1 // 2, modes, modes - M1).astype(jnp.int32)
    phases = jnp.mod(positions[:, None] * signed[None, :], length).astype(jnp.int32)
    angles = phases.astype(jnp.float32) * (2.0 * math.pi / length)
    return jnp.concatenate([jnp.cos(angles), jnp.sin(angles)], axis=1).astype(jnp.bfloat16)

def column_tables():
    modes = jnp.arange(M2, dtype=jnp.int32)
    pixels = jnp.arange(W, dtype=jnp.int32)
    phases = jnp.mod(modes[:, None] * pixels[None, :], W).astype(jnp.int32)
    angles = phases.astype(jnp.float32) * (2.0 * math.pi / W)
    return jnp.concatenate([jnp.cos(angles), -jnp.sin(angles)], axis=0).astype(jnp.bfloat16)

def inverse_rows(tables):
    cosine = tables[:, :M1]
    sine = tables[:, M1:]
    upper = jnp.concatenate([cosine.T, sine.T], axis=1)
    lower = jnp.concatenate([-sine.T, cosine.T], axis=1)
    return jnp.concatenate([upper, lower], axis=0)

def along_rows(halves, tables):
    mixed = jnp.einsum('pqch,hm->pqcm', halves.astype(jnp.float32), tables.astype(jnp.float32))
    real_part = mixed[0]
    imag_part = mixed[1]
    return jnp.concatenate([real_part[..., :M1] + imag_part[..., M1:], imag_part[..., :M1] - real_part[..., M1:]], axis=-1)

def mix_forward(spectra, weights):
    real_in, imag_in = (spectra[..., :M1], spectra[..., M1:])
    real_w, imag_w = (weights[..., :M1], weights[..., M1:])
    real_out = jnp.einsum('qck,qcok->qok', real_in, real_w) - jnp.einsum('qck,qcok->qok', imag_in, imag_w)
    imag_out = jnp.einsum('qck,qcok->qok', real_in, imag_w) + jnp.einsum('qck,qcok->qok', imag_in, real_w)
    return jnp.concatenate([real_out, imag_out], axis=-1)

def mix_backward(grads, weights):
    real_g, imag_g = (grads[..., :M1], grads[..., M1:])
    real_w, imag_w = (weights[..., :M1], weights[..., M1:])
    real_out = jnp.einsum('qok,qcok->qck', real_g, real_w) + jnp.einsum('qok,qcok->qck', imag_g, imag_w)
    imag_out = jnp.einsum('qok,qcok->qck', imag_g, real_w) - jnp.einsum('qok,qcok->qck', real_g, imag_w)
    return jnp.concatenate([real_out, imag_out], axis=-1)

def weight_term(spectra, grads):
    real_in, imag_in = (spectra[..., :M1], spectra[..., M1:])
    real_g, imag_g = (grads[..., :M1], grads[..., M1:])
    real_out = jnp.einsum('qck,qok->qcok', real_in, real_g) + jnp.einsum('qck,qok->qcok', imag_in, imag_g)
    imag_out = jnp.einsum('qck,qok->qcok', real_in, imag_g) - jnp.einsum('qck,qok->qcok', imag_in, real_g)
    return jnp.concatenate([real_out, imag_out], axis=-1)

def gelu_slope(values):
    cumulative = 0.5 * (1.0 + jax.scipy.special.erf(values / math.sqrt(2.0)))
    density = jnp.exp(-0.5 * values * values) / math.sqrt(2.0 * math.pi)
    return cumulative + values * density

def reference(inputs, cotangent, mode_weight, local_weight):
    height = TH * N_TILE
    spec_scale = 1.0 / math.sqrt(height * W)
    mode_scale = 1.0 / math.sqrt(M1 * M2)
    rows_table = row_tables(jnp.arange(height, dtype=jnp.int32), height)
    back_table = inverse_rows(rows_table).astype(jnp.float32)
    col_table = column_tables().astype(jnp.float32)
    col_three = col_table.reshape(2, M2, W)
    weights = mode_weight.astype(jnp.float32)
    local = local_weight.astype(jnp.float32)

    def to_modes(fields, scale):
        halves = jnp.einsum('qw,chw->qch', col_table, fields.astype(jnp.float32)).astype(jnp.bfloat16)
        halves = halves.reshape(2, M2, C, height)
        return (scale * along_rows(halves, rows_table)).astype(jnp.bfloat16)

    def to_pixels(spectra, scale):
        inner = jnp.einsum('qom,mj->qoj', spectra.astype(jnp.float32), back_table).astype(jnp.bfloat16)
        inner = inner.reshape(M2, C, 2, height).astype(jnp.float32)
        return scale * jnp.einsum('qoph,pqw->ohw', inner, col_three)

    def one_sample(carry, pair):
        mode_sum, local_sum = carry
        fields, grads = pair
        fields32 = fields.astype(jnp.float32)
        spectra = to_modes(fields, spec_scale)
        outputs = mix_forward(spectra.astype(jnp.float32), weights).astype(jnp.bfloat16)
        pre = to_pixels(outputs, mode_scale) + jnp.einsum('co,chw->ohw', local, fields32)
        gate_grad = (grads.astype(jnp.float32) * gelu_slope(pre)).astype(jnp.bfloat16)
        gate32 = gate_grad.astype(jnp.float32)
        local_sum = local_sum + jnp.einsum('chw,ohw->co', fields32, gate32)
        back_local = jnp.einsum('co,ohw->chw', local, gate32)
        out_grad = to_modes(gate_grad, mode_scale)
        in_grad = mix_backward(out_grad.astype(jnp.float32), weights).astype(jnp.bfloat16)
        mode_sum = mode_sum + weight_term(spectra.astype(jnp.float32), out_grad.astype(jnp.float32))
        result = (to_pixels(in_grad, spec_scale) + back_local).astype(jnp.bfloat16)
        return ((mode_sum, local_sum), result)
    start = (jnp.zeros((M2, C, C, 2 * M1), jnp.float32), jnp.zeros((C, C), jnp.float32))
    (mode_grad, local_grad), input_grad = lax.scan(one_sample, start, (inputs, cotangent))
    return (input_grad, mode_grad, local_grad)
```

```python
import math

import jax
import jax.numpy as jnp
from jax import lax
from jax.sharding import Mesh
from jax.sharding import PartitionSpec as P

C = 64
M1 = 64
M2 = 64
W = 256
TH = 16
TILE = ("tile_0", "tile_1", "tile_2")
DP = ("dp_0", "dp_1")
DP_TILE = ("dp_0", "dp_1", "tile_0", "tile_1", "tile_2")


def row_tables(positions, length):
    modes = jnp.arange(M1, dtype=jnp.int32)
    signed = jnp.where(modes < M1 // 2, modes, modes - M1)
    phases = jnp.mod(positions[:, None] * signed[None, :], length)
    angles = phases.astype(jnp.float32) * (2.0 * math.pi / length)
    return jnp.concatenate([jnp.cos(angles), jnp.sin(angles)], axis=1).astype(jnp.bfloat16)


def column_tables():
    modes = jnp.arange(M2, dtype=jnp.int32)
    pixels = jnp.arange(W, dtype=jnp.int32)
    phases = jnp.mod(modes[:, None] * pixels[None, :], W)
    angles = phases.astype(jnp.float32) * (2.0 * math.pi / W)
    return jnp.concatenate([jnp.cos(angles), -jnp.sin(angles)], axis=0).astype(jnp.bfloat16)


def inverse_rows(tables):
    cosine = tables[:, :M1]
    sine = tables[:, M1:]
    upper = jnp.concatenate([cosine.T, sine.T], axis=1)
    lower = jnp.concatenate([-sine.T, cosine.T], axis=1)
    return jnp.concatenate([upper, lower], axis=0)


def along_rows(halves, tables):
    mixed = jnp.einsum("pqsch,hm->pqscm", halves, tables, preferred_element_type=jnp.float32)
    real_part = mixed[0]
    imag_part = mixed[1]
    return jnp.concatenate(
        [real_part[..., :M1] + imag_part[..., M1:], imag_part[..., :M1] - real_part[..., M1:]],
        axis=-1,
    )


def products(left, right, form):
    return jnp.einsum(form, left, right, preferred_element_type=jnp.float32)


def mix_forward(spectra, weights):
    real_in, imag_in = (spectra[..., :M1], spectra[..., M1:])
    real_w, imag_w = (weights[..., :M1], weights[..., M1:])
    form = "qsck,qcok->qsok"
    real_out = products(real_in, real_w, form) - products(imag_in, imag_w, form)
    imag_out = products(real_in, imag_w, form) + products(imag_in, real_w, form)
    return jnp.concatenate([real_out, imag_out], axis=-1)


def mix_backward(grads, weights):
    real_g, imag_g = (grads[..., :M1], grads[..., M1:])
    real_w, imag_w = (weights[..., :M1], weights[..., M1:])
    form = "qsok,qcok->qsck"
    real_out = products(real_g, real_w, form) + products(imag_g, imag_w, form)
    imag_out = products(imag_g, real_w, form) - products(real_g, imag_w, form)
    return jnp.concatenate([real_out, imag_out], axis=-1)


def weight_term(spectra, grads):
    real_in, imag_in = (spectra[..., :M1], spectra[..., M1:])
    real_g, imag_g = (grads[..., :M1], grads[..., M1:])
    form = "qsck,qsok->qcok"
    real_out = products(real_in, real_g, form) + products(imag_in, imag_g, form)
    imag_out = products(real_in, imag_g, form) - products(imag_in, real_g, form)
    return jnp.concatenate([real_out, imag_out], axis=-1)


def gelu_slope(values):
    cumulative = 0.5 * (1.0 + jax.scipy.special.erf(values / math.sqrt(2.0)))
    density = jnp.exp(-0.5 * values * values) / math.sqrt(2.0 * math.pi)
    return cumulative + values * density


def local(inputs, cotangent, mode_weight, local_weight):
    parts = lax.axis_size(TILE)
    height = TH * parts
    owned = mode_weight.shape[0]
    spec_scale = 1.0 / math.sqrt(height * W)
    mode_scale = 1.0 / math.sqrt(M1 * M2)
    col_table = column_tables()
    col_three = col_table.reshape(2, M2, W)
    full_rows = row_tables(jnp.arange(height, dtype=jnp.int32), height)
    full_back = inverse_rows(full_rows)

    def to_owners(fields, scale):
        samples = fields.shape[0]
        halves = products(col_table, fields, "qw,schw->qsch").astype(jnp.bfloat16)
        halves = halves.reshape(2, M2, samples, C, TH)
        whole = lax.all_to_all(halves, TILE, split_axis=1, concat_axis=4, tiled=True)
        return (scale * along_rows(whole, full_rows)).astype(jnp.bfloat16)

    def to_pixels(spectra, scale):
        samples = spectra.shape[1]
        inner = products(spectra, full_back, "qsom,mj->qsoj").astype(jnp.bfloat16)
        inner = inner.reshape(owned, samples, C, 2, height)
        gathered = lax.all_to_all(inner, TILE, split_axis=4, concat_axis=0, tiled=True)
        return scale * products(gathered, col_three, "qsoph,pqw->sohw")

    spectra = to_owners(inputs, spec_scale)
    outputs = mix_forward(spectra, mode_weight).astype(jnp.bfloat16)
    pre = to_pixels(outputs, mode_scale) + products(local_weight, inputs, "co,schw->sohw")
    gate_grad = (cotangent.astype(jnp.float32) * gelu_slope(pre)).astype(jnp.bfloat16)
    local_term = products(inputs, gate_grad, "schw,sohw->co")
    back_local = products(local_weight, gate_grad, "co,sohw->schw")
    out_grad = to_owners(gate_grad, mode_scale)
    in_grad = mix_backward(out_grad, mode_weight).astype(jnp.bfloat16)
    every_x = lax.all_gather(spectra, DP, axis=1, tiled=True)
    every_g = lax.all_gather(out_grad, DP, axis=1, tiled=True)
    mode_grad = weight_term(every_x, every_g)
    result = (to_pixels(in_grad, spec_scale) + back_local).astype(jnp.bfloat16)
    local_grad = lax.psum(local_term, DP_TILE)
    return (result, mode_grad, local_grad)


def solution(mesh):
    finer = Mesh(
        mesh.devices.reshape(2, 2, 2, 4, 8), ("dp_0", "dp_1", "tile_0", "tile_1", "tile_2")
    )
    in_specs = (P(DP, None, TILE, None), P(DP, None, TILE, None), P(TILE, None, None, None), P())
    out_specs = (P(DP, None, TILE, None), P(TILE, None, None, None), P())
    return jax.shard_map(local, mesh=finer, in_specs=in_specs, out_specs=out_specs, check_vma=False)
```

```python
import math

import jax
import jax.numpy as jnp
import numpy as np
from jax import lax
from jax.experimental import pallas as pl
from jax.experimental.pallas import tpu as pltpu
from jax.sharding import PartitionSpec as P

C = 64
M1 = 64
M2 = 64
W = 256
TH = 16
H = 1024
N_TILE = 64
N_DP = 4
S = 2
RH = 8
RL = 2
SPEC = 1.0 / math.sqrt(H * W)
MODE = 1.0 / math.sqrt(M1 * M2)
F32 = jnp.float32
BF16 = jnp.bfloat16
MESH = pl.DeviceIdType.MESH


def column_rows():
    phase = np.mod(np.arange(M2)[:, None] * np.arange(W)[None, :], W) * (2.0 * math.pi / W)
    return np.stack([np.cos(phase), -np.sin(phase)], axis=1).reshape(2 * M2, W)


def row_maps():
    modes = np.arange(M1)
    signed = np.where(modes < M1 // 2, modes, modes - M1)
    phase = np.mod(np.arange(H)[:, None] * signed[None, :], H) * (2.0 * math.pi / H)
    cosine = np.cos(phase).reshape(N_TILE, RH, RL, M1)
    sine = np.sin(phase).reshape(N_TILE, RH, RL, M1)
    first = np.concatenate([cosine, -sine], axis=-1)
    second = np.concatenate([sine, cosine], axis=-1)
    return np.stack([first, second], axis=1).reshape(N_TILE * 2 * RH, RL * 2 * M1)


def mm(left, right):
    return lax.dot_general(left, right, (((1,), (0,)), ((), ())), preferred_element_type=F32)


def mm_nt(left, right):
    return lax.dot_general(left, right, (((1,), (1,)), ((), ())), preferred_element_type=F32)


def gelu_slope(values):
    cumulative = 0.5 * (1.0 + lax.erf(values * (1.0 / math.sqrt(2.0))))
    density = jnp.exp(-0.5 * values * values) * (1.0 / math.sqrt(2.0 * math.pi))
    return cumulative + values * density


def kernel(v_hbm, ct_hbm, w_hbm, mix_hbm, col_hbm, inv_hbm, fwd_hbm,
           og_hbm, mg_hbm, lg_hbm,
           v, ct, w16, w32, wt32, mix, col, inv, fwd, m32, b32, gg, og, snd, rcv,
           xs, ds, xall, dall, pa, pb, x1, x2, d1, d2, mg, lga, lgs, lg1, lgr, lgp, lgd, lge, lgf,
           load_sem, send_sem, recv_sem, dp_send, dp_recv, lg_send, lg_recv, out_sem):
    me = lax.axis_index("tile")
    my = lax.axis_index("dp")
    me_y, me_x, me_z = lax.div(me, 32), lax.rem(lax.div(me, 8), 4), lax.rem(me, 8)

    def partner(i):
        j, k = lax.div(i, 8), lax.rem(i, 8)
        kx = lax.rem(k, 4)
        dz = 4 + (1 - 2 * lax.rem(j, 2)) * lax.div(j + 1, 2)
        dx = 2 + (1 - 2 * lax.rem(kx, 2)) * lax.div(kx + 1, 2)
        dy = 1 - lax.div(k, 4)
        return lax.rem(me_y + dy, 2) * 32 + lax.rem(me_x + dx, 4) * 8 + lax.rem(me_z + dz, 8)

    def group(j):
        return lax.rem(my + j, N_DP)

    loads = [
        pltpu.make_async_copy(a, b, load_sem.at[n])
        for n, (a, b) in enumerate([
            (col_hbm, col), (v_hbm.at[0], v.at[0]), (v_hbm.at[1], v.at[1]), (fwd_hbm, fwd),
            (w_hbm, w16), (inv_hbm, inv), (mix_hbm, mix), (ct_hbm, ct)])
    ]
    for copy in loads:
        copy.start()

    barrier = pltpu.get_barrier_semaphore()

    def greet(i, carry):
        pl.semaphore_signal(barrier, inc=1, device_id={"tile": partner(i)}, device_id_type=MESH)
        return carry

    lax.fori_loop(0, N_TILE - 1, greet, 0)
    for j in range(1, N_DP):
        pl.semaphore_signal(barrier, inc=1, device_id={"dp": group(j)}, device_id_type=MESH)

    lane = lax.broadcasted_iota(jnp.int32, (C, 128), 1)
    low = lane < 64
    sgn = jnp.where(low, 1.0, -1.0).astype(F32)

    def exchange(phase, s):
        def send(i, carry):
            p = partner(i)
            pltpu.make_async_remote_copy(
                src_ref=snd.at[phase, s, pl.ds(pl.multiple_of(p * 16, 16), 16), :],
                dst_ref=rcv.at[phase, s, pl.ds(pl.multiple_of(me * 16, 16), 16), :],
                send_sem=send_sem.at[phase, s], recv_sem=recv_sem.at[phase, s],
                device_id={"tile": p}, device_id_type=MESH).start()
            return carry

        lax.fori_loop(0, N_TILE - 1, send, 0)
        mine = pl.ds(pl.multiple_of(me * 16, 16), 16)
        pltpu.make_async_copy(
            snd.at[phase, s, mine, :], rcv.at[phase, s, mine, :], recv_sem.at[phase, s]).start()

    def arrived(phase, s):
        pltpu.make_async_copy(rcv.at[phase, s], rcv.at[phase, s], recv_sem.at[phase, s]).wait()

    def to_group(src, dst, s, n):
        for j in range(1, N_DP):
            pltpu.make_async_remote_copy(
                src_ref=src.at[s], dst_ref=dst.at[my, s], send_sem=dp_send.at[n], recv_sem=dp_recv.at[n],
                device_id={"dp": group(j)}, device_id_type=MESH).start()
        pltpu.make_async_copy(src.at[s], dst.at[my, s], dp_recv.at[n]).start()

    def pack(phase, s):
        snd[phase, s] = m32[...].astype(BF16)

    loads[0].wait()
    for s in range(S):
        loads[1 + s].wait()

        def column(r, carry):
            tile = v[s, pl.ds(pl.multiple_of(r * 128, 128), 128), :]
            m32[pl.ds(r, 128, stride=RH), :] = mm_nt(col[...], tile)
            return carry

        lax.fori_loop(0, RH, column, 0)
        pack(0, s)
        if s == 0:
            pl.semaphore_wait(barrier, N_TILE - 1 + N_DP - 1)
        exchange(0, s)

    loads[4].wait()

    def widen(c, carry):
        at = pl.ds(pl.multiple_of(c * 64, 64), 64)
        w32[at, :] = w16[at, :].astype(F32)
        return carry

    lax.fori_loop(0, C, widen, 0)

    def spectrum(phase, s, scale):
        both = mm(fwd[...], rcv[phase, s])
        turned = (both[:128] + pltpu.roll(both[128:], 64, 1)).T
        return (turned[:64] * scale).astype(BF16)

    def halves(value):
        wide = value.astype(F32)
        other = pltpu.roll(wide, 64, 1)
        pa[...] = jnp.where(low, wide, other)
        pb[...] = jnp.where(low, other, wide)

    def mix_rows(table):
        def step(c, carry):
            first, second = carry
            block = table[pl.ds(pl.multiple_of(c * 64, 64), 64), :]
            return first + pa[pl.ds(c, 1), :] * block, second + pb[pl.ds(c, 1), :] * block

        zero = jnp.zeros((C, 128), F32)
        return lax.fori_loop(0, C, step, (zero, zero), unroll=4)

    def back_to_rows(phase, s, value, scale):
        small = (value.astype(BF16).astype(F32) * scale).astype(BF16)
        none = jnp.zeros_like(small)
        right = jnp.concatenate(
            [jnp.concatenate([small, none], axis=1), jnp.concatenate([none, small], axis=1)], axis=0)

        def rows(n, carry):
            at = pl.ds(pl.multiple_of(n * 256, 256), 256)
            snd[phase, s, at, :] = mm_nt(inv[at, :], right).astype(BF16)
            return carry

        lax.fori_loop(0, 4, rows, 0)
        exchange(phase, s)

    loads[3].wait()
    loads[5].wait()
    for s in range(S):
        arrived(0, s)
        xs[s] = spectrum(0, s, SPEC)
        to_group(xs, xall, s, 0)
        halves(xs[s])
        first, second = mix_rows(w32)
        back_to_rows(1, s, first - sgn * pltpu.roll(second, 64, 1), MODE)

    def swap(o, carry):
        wt32[pl.ds(pl.multiple_of(o * 64, 64), 64), :] = w32[pl.ds(o, 64, stride=64), :]
        return carry

    lax.fori_loop(0, C, swap, 0)
    loads[6].wait()
    loads[7].wait()
    lga[...] = jnp.zeros_like(lga)

    for s in range(S):
        arrived(1, s)
        b32[...] = rcv[1, s].astype(F32)

        def gate(r, carry):
            at = pl.ds(pl.multiple_of(r * 128, 128), 128)
            spectral = b32[pl.ds(r, 128, stride=RH), :].T.astype(BF16)
            tile = v[s, at, :]
            pre = mm(spectral, col[...]) + mm(mix[0], tile)
            grad = (ct[s, at, :].astype(F32) * gelu_slope(pre)).astype(BF16)
            gg[s, at, :] = grad
            m32[pl.ds(r, 128, stride=RH), :] = mm_nt(col[...], grad)
            lga[...] += mm_nt(tile, grad)
            return carry

        lax.fori_loop(0, RH, gate, 0)
        pack(2, s)
        exchange(2, s)

    lgs[...] = lga[:64] + pltpu.roll(lga[64:], 64, 1)

    def spread(c, carry):
        lg1[c] = lgs[pl.ds(c, 1), :]
        return carry

    lax.fori_loop(0, C, spread, 0)

    def send_rows(src_of, dst, n):
        def send(i, carry):
            p = partner(i)
            pltpu.make_async_remote_copy(
                src_ref=src_of(p), dst_ref=dst.at[me], send_sem=lg_send.at[n], recv_sem=lg_recv.at[n],
                device_id={"tile": p}, device_id_type=MESH).start()
            return carry

        lax.fori_loop(0, N_TILE - 1, send, 0)
        pltpu.make_async_copy(src_of(me), dst.at[me], lg_recv.at[n]).start()

    send_rows(lambda p: lg1.at[p], lgr, 0)

    for s in range(S):
        arrived(2, s)
        ds[s] = spectrum(2, s, MODE)
        to_group(ds, dall, s, 1)
        halves(ds[s])
        first, second = mix_rows(wt32)
        back_to_rows(3, s, pltpu.roll(second, 64, 1) + sgn * first, SPEC)

    pltpu.make_async_copy(lgr, lgr, lg_recv.at[0]).wait()
    lgp[0] = jnp.sum(lgr[...], axis=0)
    for j in range(1, N_DP):
        pltpu.make_async_remote_copy(
            src_ref=lgp.at[0], dst_ref=lgd.at[my], send_sem=lg_send.at[2], recv_sem=lg_recv.at[2],
            device_id={"dp": group(j)}, device_id_type=MESH).start()
    pltpu.make_async_copy(lgp.at[0], lgd.at[my], lg_recv.at[2]).start()

    pltpu.make_async_copy(xall, xall, dp_recv.at[0]).wait()
    pltpu.make_async_copy(dall, dall, dp_recv.at[1]).wait()
    for g in range(N_DP):
        for s in range(S):
            n = g * S + s
            wide = xall[g, s].astype(F32)
            other = pltpu.roll(wide, 64, 1)
            x1[n] = jnp.where(low, wide, other)
            x2[n] = jnp.where(low, other, -wide)
            grad = dall[g, s].astype(F32)
            d1[n] = grad
            d2[n] = pltpu.roll(grad, 64, 1)

    pltpu.make_async_copy(lgd, lgd, lg_recv.at[2]).wait()
    lge[0] = jnp.sum(lgd[...], axis=0)
    send_rows(lambda p: lge.at[0], lgf, 1)

    def outer(c, carry):
        even = jnp.zeros((C, 128), F32)
        odd = jnp.zeros((C, 128), F32)
        for n in range(N_DP * S):
            first, second = d1[n], d2[n]
            even += x1[n, pl.ds(2 * c, 1), :] * first + x2[n, pl.ds(2 * c, 1), :] * second
            odd += x1[n, pl.ds(2 * c + 1, 1), :] * first + x2[n, pl.ds(2 * c + 1, 1), :] * second
        at = pl.multiple_of(c * 128, 128)
        mg[pl.ds(at, 64), :] = even
        mg[pl.ds(at + 64, 64), :] = odd
        pltpu.make_async_copy(mg.at[pl.ds(at, 128), :], mg_hbm.at[pl.ds(at, 128), :], out_sem.at[0]).start()
        return carry

    lax.fori_loop(0, C // 2, outer, 0)

    for s in range(S):
        arrived(3, s)
        b32[...] = rcv[3, s].astype(F32)

        def back(r, carry):
            at = pl.ds(pl.multiple_of(r * 128, 128), 128)
            spectral = b32[pl.ds(r, 128, stride=RH), :].T.astype(BF16)
            og[s, at, :] = (mm(spectral, col[...]) + mm(mix[1], gg[s, at, :])).astype(BF16)
            pltpu.make_async_copy(og.at[s, at, :], og_hbm.at[s, at, :], out_sem.at[1]).start()
            return carry

        lax.fori_loop(0, RH, back, 0)

    pltpu.make_async_copy(lgf, lgf, lg_recv.at[1]).wait()
    tail = pltpu.make_async_copy(lgf, lg_hbm, out_sem.at[2])
    tail.start()

    for phase in range(4):
        for s in range(S):
            sent = snd.at[phase, s, pl.ds(0, 16 * (N_TILE - 1)), :]
            pltpu.make_async_copy(sent, sent, send_sem.at[phase, s]).wait()
    for n, ref in ((0, xall), (1, dall)):
        sent = ref.at[pl.ds(0, N_DP - 1)]
        pltpu.make_async_copy(sent, sent, dp_send.at[n]).wait()
    for n in range(2):
        sent = lgr.at[pl.ds(0, N_TILE - 1)]
        pltpu.make_async_copy(sent, sent, lg_send.at[n]).wait()
    sent = lgd.at[pl.ds(0, N_DP - 1)]
    pltpu.make_async_copy(sent, sent, lg_send.at[2]).wait()
    pltpu.make_async_copy(mg, mg_hbm, out_sem.at[0]).wait()
    pltpu.make_async_copy(og, og_hbm, out_sem.at[1]).wait()
    tail.wait()


def step(inputs, cotangent, mode_weight, local_weight):
    def row_major(field):
        return jnp.swapaxes(field, 1, 2).reshape(S, TH * C, W)

    paired = jnp.tile(local_weight, (2, 2))
    same = jnp.asarray(np.kron(np.eye(2), np.ones((C, C))).astype(bool))
    mixes = jnp.where(same[None], jnp.stack([paired.T, paired]), jnp.zeros((), BF16))
    rows = row_maps()
    col = jnp.asarray(column_rows(), BF16)
    inv = jnp.asarray(rows, BF16)
    fwd = jnp.asarray(np.ascontiguousarray(rows.T), BF16)
    dma = pltpu.SemaphoreType.DMA
    vm = pltpu.VMEM
    og, mg, lg = pl.pallas_call(
        kernel,
        out_shape=(
            jax.ShapeDtypeStruct((S, TH * C, W), BF16),
            jax.ShapeDtypeStruct((C * C, 2 * M1), F32),
            jax.ShapeDtypeStruct((C, 1, 128), F32),
        ),
        in_specs=[pl.BlockSpec(memory_space=pl.ANY)] * 7,
        out_specs=(pl.BlockSpec(memory_space=pl.ANY),) * 3,
        scratch_shapes=[
            vm((S, TH * C, W), BF16), vm((S, TH * C, W), BF16),
            vm((C * C, 128), BF16), vm((C * C, 128), F32), vm((C * C, 128), F32),
            vm((2, 128, 128), BF16), vm((128, W), BF16), vm((1024, 256), BF16), vm((256, 1024), BF16),
            vm((1024, 128), F32), vm((1024, 128), F32),
            vm((S, TH * C, W), BF16), vm((S, TH * C, W), BF16),
            vm((4, S, 1024, 128), BF16), vm((4, S, 1024, 128), BF16),
            vm((S, C, 128), BF16), vm((S, C, 128), BF16),
            vm((N_DP, S, C, 128), BF16), vm((N_DP, S, C, 128), BF16),
            vm((C, 128), F32), vm((C, 128), F32),
            vm((N_DP * S, C, 128), F32), vm((N_DP * S, C, 128), F32),
            vm((N_DP * S, C, 128), F32), vm((N_DP * S, C, 128), F32),
            vm((C * C, 128), F32),
            vm((128, 128), F32), vm((C, 128), F32),
            vm((C, 1, 128), F32), vm((C, 1, 128), F32), vm((1, 1, 128), F32), vm((N_DP, 1, 128), F32),
            vm((1, 1, 128), F32), vm((C, 1, 128), F32),
            dma((8,)), dma((4, S)), dma((4, S)), dma((2,)), dma((2,)), dma((3,)), dma((3,)), dma((3,)),
        ],
        compiler_params=pltpu.CompilerParams(
            collective_id=0, has_side_effects=True, vmem_limit_bytes=48 << 20),
    )(row_major(inputs), row_major(cotangent), mode_weight.reshape(C * C, 2 * M1), mixes, col, inv, fwd)
    input_grad = jnp.swapaxes(og.reshape(S, TH, C, W), 1, 2)
    return input_grad, mg.reshape(1, C, C, 2 * M1), lg[:, 0, :C]


def solution(mesh):
    in_specs = (P("dp", None, "tile", None), P("dp", None, "tile", None), P("tile", None, None, None), P())
    out_specs = (P("dp", None, "tile", None), P("tile", None, None, None), P())
    return jax.shard_map(step, mesh=mesh, in_specs=in_specs, out_specs=out_specs, check_vma=False)
```

```python
import math

import jax
import jax.numpy as jnp
import numpy as np
from jax import lax
from jax.experimental import pallas as pl
from jax.experimental.pallas import tpu as pltpu
from jax.sharding import PartitionSpec as P

C = 64
M1 = 64
M2 = 64
W = 256
TH = 16
H = 1024
N_TILE = 64
N_DP = 4
S = 2
RH = 8
RL = 2
FAR_FIRST = (4, 3, 5, 2, 6, 1, 7, 0)
SPEC = 1.0 / math.sqrt(H * W)
MODE = 1.0 / math.sqrt(M1 * M2)
F32 = jnp.float32
BF16 = jnp.bfloat16
MESH = pl.DeviceIdType.MESH


def column_rows():
    phase = np.mod(np.arange(M2)[:, None] * np.arange(W)[None, :], W) * (2.0 * math.pi / W)
    return np.stack([np.cos(phase), -np.sin(phase)], axis=1).reshape(2 * M2, W)


def row_maps():
    modes = np.arange(M1)
    signed = np.where(modes < M1 // 2, modes, modes - M1)
    phase = np.mod(np.arange(H)[:, None] * signed[None, :], H) * (2.0 * math.pi / H)
    cosine = np.cos(phase).reshape(N_TILE, RH, RL, M1)
    sine = np.sin(phase).reshape(N_TILE, RH, RL, M1)
    first = np.concatenate([cosine, -sine], axis=-1)
    second = np.concatenate([sine, cosine], axis=-1)
    return np.stack([first, second], axis=1).reshape(N_TILE * 2 * RH, RL * 2 * M1)


def mm(left, right):
    return lax.dot_general(left, right, (((1,), (0,)), ((), ())), preferred_element_type=F32)


def mm_nt(left, right):
    return lax.dot_general(left, right, (((1,), (1,)), ((), ())), preferred_element_type=F32)


def gelu_slope(values):
    cumulative = 0.5 * (1.0 + lax.erf(values * (1.0 / math.sqrt(2.0))))
    density = jnp.exp(-0.5 * values * values) * (1.0 / math.sqrt(2.0 * math.pi))
    return cumulative + values * density


def input_gradient(received, grad, mix, col, b32, wide, result):
    b32[...] = received[...].astype(F32)

    def back(r, carry):
        spectral = b32[pl.ds(r, 128, stride=RH), :].T.astype(BF16)
        value = mm(spectral, col[...]) + mm(mix[...], grad[pl.ds(pl.multiple_of(r * 128, 128), 128), :])
        for n in range(RL):
            for half in range(2):
                wide[half, pl.ds(2 * r + n, C, stride=TH), :] = value[n * C:(n + 1) * C, half * 128:(half + 1) * 128]
        return carry

    lax.fori_loop(0, RH, back, 0, unroll=2)
    for half in range(2):
        result[:, half * 128:(half + 1) * 128] = wide[half].astype(BF16)


def finish(og0, mg, lg, last, ggl, mixl, coll, og_hbm, mg_hbm, lg_hbm, b32, wide, og1, sem):
    copies = [
        pltpu.make_async_copy(a, b, sem.at[n])
        for n, (a, b) in enumerate([(mg, mg_hbm), (og0, og_hbm.at[0]), (lg, lg_hbm), (og1, og_hbm.at[1])])
    ]
    for copy in copies[:3]:
        copy.start()
    input_gradient(last, ggl, mixl, coll, b32, wide, og1)
    copies[3].start()
    for copy in copies:
        copy.wait()


def kernel(v_hbm, ct_hbm, w_hbm, l_hbm, col_hbm, inv_hbm, fwd_hbm,
           og, mg, lg, last, ggl, mixl, coll,
           v, vn, v32, ctn, ct, w16, w32, wt32, l16, mix, col, inv, fwd, m32, b32, gg, snd, rcv,
           xs, ds, xall, dall, pa, pb, x1, x2, d1, d2, lga, lgs, lg1, lgr, lgp, lgd, lge, lgf,
           load_sem, send_sem, recv_sem, dp_send, dp_recv, lg_send, lg_recv):
    me = lax.axis_index("tile")
    my = lax.axis_index("dp")
    me_y, me_x, me_z = lax.div(me, 32), lax.rem(lax.div(me, 8), 4), lax.rem(me, 8)

    column_of = [lax.rem(me_z + dz, 8) for dz in range(8)]

    def plane(k):
        kx = lax.rem(k, 4)
        dx = 2 + (1 - 2 * lax.rem(kx, 2)) * lax.div(kx + 1, 2)
        dy = 1 - lax.div(k, 4)
        return lax.rem(me_y + dy, 2) * 32 + lax.rem(me_x + dx, 4) * 8

    def to_others(send):
        def planes(k, carry):
            base = plane(k)
            for dz in FAR_FIRST:
                send(base + column_of[dz])
            return carry

        lax.fori_loop(0, 7, planes, 0)
        for dz in FAR_FIRST[:-1]:
            send(me_y * 32 + me_x * 8 + column_of[dz])

    def group(j):
        return lax.rem(my + j, N_DP)

    loads = [
        pltpu.make_async_copy(a, b, load_sem.at[n])
        for n, (a, b) in enumerate([
            (col_hbm, col), (v_hbm.at[0], vn.at[0]), (v_hbm.at[1], vn.at[1]), (fwd_hbm, fwd),
            (w_hbm, w16), (inv_hbm, inv), (l_hbm, l16), (ct_hbm, ctn)])
    ]
    for copy in loads:
        copy.start()

    barrier = pltpu.get_barrier_semaphore()

    def greet(p):
        pl.semaphore_signal(barrier, inc=1, device_id={"tile": p}, device_id_type=MESH)

    to_others(greet)
    for j in range(1, N_DP):
        pl.semaphore_signal(barrier, inc=1, device_id={"dp": group(j)}, device_id_type=MESH)

    lane = lax.broadcasted_iota(jnp.int32, (C, 128), 1)
    low = lane < 64
    sgn = jnp.where(low, 1.0, -1.0).astype(F32)

    def exchange(phase, s):
        def send(p):
            pltpu.make_async_remote_copy(
                src_ref=snd.at[phase, s, pl.ds(pl.multiple_of(p * 16, 16), 16), :],
                dst_ref=rcv.at[phase, s, pl.ds(pl.multiple_of(me * 16, 16), 16), :],
                send_sem=send_sem.at[phase, s], recv_sem=recv_sem.at[phase, s],
                device_id={"tile": p}, device_id_type=MESH).start()

        to_others(send)
        mine = pl.ds(pl.multiple_of(me * 16, 16), 16)
        pltpu.make_async_copy(
            snd.at[phase, s, mine, :], rcv.at[phase, s, mine, :], recv_sem.at[phase, s]).start()

    def arrived(phase, s):
        pltpu.make_async_copy(rcv.at[phase, s], rcv.at[phase, s], recv_sem.at[phase, s]).wait()

    def to_group(src, dst, s, n):
        for j in range(1, N_DP):
            pltpu.make_async_remote_copy(
                src_ref=src.at[s], dst_ref=dst.at[my, s], send_sem=dp_send.at[n], recv_sem=dp_recv.at[n],
                device_id={"dp": group(j)}, device_id_type=MESH).start()
        pltpu.make_async_copy(src.at[s], dst.at[my, s], dp_recv.at[n]).start()

    def pack(phase, s):
        snd[phase, s] = m32[...].astype(BF16)

    def rows_of(natural, r):
        return jnp.concatenate([
            jnp.concatenate([natural[half, pl.ds(2 * r + n, C, stride=TH), :] for half in range(2)], axis=1)
            for n in range(RL)], axis=0)

    def widen_into(natural, source):
        for half in range(2):
            natural[half] = source[:, half * 128:(half + 1) * 128].astype(F32)

    loads[0].wait()
    for s in range(S):
        loads[1 + s].wait()

        def column(r, carry):
            tile = rows_of(v32, r).astype(BF16)
            v[s, pl.ds(pl.multiple_of(r * 128, 128), 128), :] = tile
            m32[pl.ds(r, 128, stride=RH), :] = mm_nt(col[...], tile)
            return carry

        widen_into(v32, vn.at[s])
        lax.fori_loop(0, RH, column, 0, unroll=2)
        pack(0, s)
        if s == 0:
            pl.semaphore_wait(barrier, N_TILE - 1 + N_DP - 1)
        exchange(0, s)

    loads[4].wait()

    def widen(c, carry):
        at = pl.ds(pl.multiple_of(c * 64, 64), 64)
        w32[at, :] = w16[at, :].astype(F32)
        return carry

    lax.fori_loop(0, C, widen, 0, unroll=4)
    loads[6].wait()
    mix[...] = jnp.zeros_like(mix)
    pointwise = l16[...].astype(F32)
    mix[0, :64, :64] = pointwise.T
    mix[0, 64:, 64:] = pointwise.T
    mix[1, :64, :64] = pointwise
    mix[1, 64:, 64:] = pointwise
    loads[7].wait()
    for s in range(S):
        widen_into(ct.at[s], ctn.at[s])

    def spectrum(phase, s, scale):
        both = mm(fwd[...], rcv[phase, s])
        turned = (both[:128] + pltpu.roll(both[128:], 64, 1)).T
        return (turned[:64] * scale).astype(BF16)

    def halves(value):
        wide = value.astype(F32)
        other = pltpu.roll(wide, 64, 1)
        pa[...] = jnp.where(low, wide, other)
        pb[...] = jnp.where(low, other, wide)

    def mix_rows(table):
        def step(c, carry):
            first, second = carry
            block = table[pl.ds(pl.multiple_of(c * 64, 64), 64), :]
            return first + pa[pl.ds(c, 1), :] * block, second + pb[pl.ds(c, 1), :] * block

        zero = jnp.zeros((C, 128), F32)
        return lax.fori_loop(0, C, step, (zero, zero), unroll=4)

    def back_to_rows(phase, s, value, scale):
        small = value.astype(BF16).astype(F32) * scale
        none = jnp.zeros((C, 128), F32)
        right = jnp.concatenate(
            [jnp.concatenate([small, none], axis=1), jnp.concatenate([none, small], axis=1)], axis=0).T.astype(BF16)

        def rows(n, carry):
            at = pl.ds(pl.multiple_of(n * 256, 256), 256)
            snd[phase, s, at, :] = mm(inv[at, :], right).astype(BF16)
            return carry

        lax.fori_loop(0, 4, rows, 0)
        exchange(phase, s)

    loads[3].wait()
    loads[5].wait()
    for s in range(S):
        arrived(0, s)
        xs[s] = spectrum(0, s, SPEC)
        to_group(xs, xall, s, 0)
        halves(xs[s])
        first, second = mix_rows(w32)
        back_to_rows(1, s, first - sgn * pltpu.roll(second, 64, 1), MODE)

    def swap(o, carry):
        wt32[pl.ds(pl.multiple_of(o * 64, 64), 64), :] = w32[pl.ds(o, 64, stride=64), :]
        return carry

    lax.fori_loop(0, C, swap, 0)
    lga[...] = jnp.zeros_like(lga)

    for s in range(S):
        arrived(1, s)
        b32[...] = rcv[1, s].astype(F32)

        def gate(r, carry):
            at = pl.ds(pl.multiple_of(r * 128, 128), 128)
            spectral = b32[pl.ds(r, 128, stride=RH), :].T.astype(BF16)
            tile = v[s, at, :]
            pre = mm(spectral, col[...]) + mm(mix[0].astype(BF16), tile)
            grad = (rows_of(ct.at[s], r) * gelu_slope(pre)).astype(BF16)
            gg[s, at, :] = grad
            m32[pl.ds(r, 128, stride=RH), :] = mm_nt(col[...], grad)
            lga[...] += mm_nt(tile, grad)
            return carry

        lax.fori_loop(0, RH, gate, 0, unroll=2)
        pack(2, s)
        exchange(2, s)

    lgs[...] = lga[:64] + pltpu.roll(lga[64:], 64, 1)

    def spread(c, carry):
        lg1[c] = lgs[pl.ds(c, 1), :]
        return carry

    lax.fori_loop(0, C, spread, 0)

    def send_rows(src_of, dst, n):
        def send(p):
            pltpu.make_async_remote_copy(
                src_ref=src_of(p), dst_ref=dst.at[me], send_sem=lg_send.at[n], recv_sem=lg_recv.at[n],
                device_id={"tile": p}, device_id_type=MESH).start()

        to_others(send)
        pltpu.make_async_copy(src_of(me), dst.at[me], lg_recv.at[n]).start()

    send_rows(lambda p: lg1.at[p], lgr, 0)

    for s in range(S):
        arrived(2, s)
        ds[s] = spectrum(2, s, MODE)
        to_group(ds, dall, s, 1)
        halves(ds[s])
        first, second = mix_rows(wt32)
        back_to_rows(3, s, pltpu.roll(second, 64, 1) + sgn * first, SPEC)

    pltpu.make_async_copy(lgr, lgr, lg_recv.at[0]).wait()
    lgp[0] = jnp.sum(lgr[...], axis=0)
    for j in range(1, N_DP):
        pltpu.make_async_remote_copy(
            src_ref=lgp.at[0], dst_ref=lgd.at[my], send_sem=lg_send.at[2], recv_sem=lg_recv.at[2],
            device_id={"dp": group(j)}, device_id_type=MESH).start()
    pltpu.make_async_copy(lgp.at[0], lgd.at[my], lg_recv.at[2]).start()

    pltpu.make_async_copy(xall, xall, dp_recv.at[0]).wait()
    pltpu.make_async_copy(dall, dall, dp_recv.at[1]).wait()
    for g in range(N_DP):
        for s in range(S):
            n = g * S + s
            wide = xall[g, s].astype(F32)
            other = pltpu.roll(wide, 64, 1)
            x1[n] = jnp.where(low, wide, other)
            x2[n] = jnp.where(low, other, -wide)
            grad = dall[g, s].astype(F32)
            d1[n] = grad
            d2[n] = pltpu.roll(grad, 64, 1)

    pltpu.make_async_copy(lgd, lgd, lg_recv.at[2]).wait()
    lge[0] = jnp.sum(lgd[...], axis=0)
    send_rows(lambda p: lge.at[0], lgf, 1)

    def outer(c, carry):
        even = jnp.zeros((C, 128), F32)
        odd = jnp.zeros((C, 128), F32)
        for n in range(N_DP * S):
            first, second = d1[n], d2[n]
            even += x1[n, pl.ds(2 * c, 1), :] * first + x2[n, pl.ds(2 * c, 1), :] * second
            odd += x1[n, pl.ds(2 * c + 1, 1), :] * first + x2[n, pl.ds(2 * c + 1, 1), :] * second
        at = pl.multiple_of(c * 128, 128)
        mg[pl.ds(at, 64), :] = even
        mg[pl.ds(at + 64, 64), :] = odd
        return carry

    lax.fori_loop(0, C // 2, outer, 0)

    mixl[...] = mix[1].astype(BF16)
    coll[...] = col[...]
    ggl[...] = gg[1]
    arrived(3, 0)
    input_gradient(rcv.at[3, 0], gg.at[0], mixl, col, b32, v32, og)

    pltpu.make_async_copy(lgf, lgf, lg_recv.at[1]).wait()

    def gather(c, carry):
        lgs[pl.ds(c, 1), :] = lgf[c]
        return carry

    lax.fori_loop(0, C, gather, 0)
    lg[...] = lgs[:, :C]
    arrived(3, 1)
    last[...] = rcv[3, 1]

    for phase in range(4):
        for s in range(S):
            sent = snd.at[phase, s, pl.ds(0, 16 * (N_TILE - 1)), :]
            pltpu.make_async_copy(sent, sent, send_sem.at[phase, s]).wait()
    for n, ref in ((0, xall), (1, dall)):
        sent = ref.at[pl.ds(0, N_DP - 1)]
        pltpu.make_async_copy(sent, sent, dp_send.at[n]).wait()
    for n in range(2):
        sent = lgr.at[pl.ds(0, N_TILE - 1)]
        pltpu.make_async_copy(sent, sent, lg_send.at[n]).wait()
    sent = lgd.at[pl.ds(0, N_DP - 1)]
    pltpu.make_async_copy(sent, sent, lg_send.at[2]).wait()


def step(inputs, cotangent, mode_weight, local_weight):
    rows = row_maps()
    col = jnp.asarray(column_rows(), BF16)
    inv = jnp.asarray(rows, BF16)
    fwd = jnp.asarray(np.ascontiguousarray(rows.T), BF16)
    dma = pltpu.SemaphoreType.DMA
    vm = pltpu.VMEM
    here = pl.BlockSpec(memory_space=pltpu.VMEM)
    anywhere = pl.BlockSpec(memory_space=pl.ANY)
    ready = pl.pallas_call(
        kernel,
        out_shape=(
            jax.ShapeDtypeStruct((C * TH, W), BF16),
            jax.ShapeDtypeStruct((C * C, 2 * M1), F32),
            jax.ShapeDtypeStruct((C, C), F32),
            jax.ShapeDtypeStruct((1024, 128), BF16),
            jax.ShapeDtypeStruct((TH * C, W), BF16),
            jax.ShapeDtypeStruct((128, 128), BF16),
            jax.ShapeDtypeStruct((128, W), BF16),
        ),
        in_specs=[anywhere] * 7,
        out_specs=(here,) * 7,
        scratch_shapes=[
            vm((S, TH * C, W), BF16), vm((S, TH * C, W), BF16), vm((2, TH * C, 128), F32),
            vm((S, TH * C, W), BF16), vm((S, 2, TH * C, 128), F32),
            vm((C * C, 128), BF16), vm((C * C, 128), F32), vm((C * C, 128), F32),
            vm((C, C), BF16), vm((2, 128, 128), F32), vm((128, W), BF16), vm((1024, 256), BF16), vm((256, 1024), BF16),
            vm((1024, 128), F32), vm((1024, 128), F32),
            vm((S, TH * C, W), BF16),
            vm((4, S, 1024, 128), BF16), vm((4, S, 1024, 128), BF16),
            vm((S, C, 128), BF16), vm((S, C, 128), BF16),
            vm((N_DP, S, C, 128), BF16), vm((N_DP, S, C, 128), BF16),
            vm((C, 128), F32), vm((C, 128), F32),
            vm((N_DP * S, C, 128), F32), vm((N_DP * S, C, 128), F32),
            vm((N_DP * S, C, 128), F32), vm((N_DP * S, C, 128), F32),
            vm((128, 128), F32), vm((C, 128), F32),
            vm((C, 1, 128), F32), vm((C, 1, 128), F32), vm((1, 1, 128), F32), vm((N_DP, 1, 128), F32),
            vm((1, 1, 128), F32), vm((C, 1, 128), F32),
            dma((8,)), dma((4, S)), dma((4, S)), dma((2,)), dma((2,)), dma((3,)), dma((3,)),
        ],
        compiler_params=pltpu.CompilerParams(
            collective_id=0, has_side_effects=True, vmem_limit_bytes=40 << 20),
    )(*[pltpu.with_memory_space_constraint(a, pltpu.HBM) for a in (
        inputs.reshape(S, C * TH, W), cotangent.reshape(S, C * TH, W), mode_weight.reshape(C * C, 2 * M1),
        local_weight, col, inv, fwd)])
    og, mg, lg = pl.pallas_call(
        finish,
        out_shape=(
            jax.ShapeDtypeStruct((S, C * TH, W), BF16),
            jax.ShapeDtypeStruct((C * C, 2 * M1), F32),
            jax.ShapeDtypeStruct((C, C), F32),
        ),
        in_specs=[anywhere, anywhere, anywhere, here, here, here, here],
        out_specs=(anywhere,) * 3,
        scratch_shapes=[vm((1024, 128), F32), vm((2, TH * C, 128), F32), vm((C * TH, W), BF16), dma((4,))],
        compiler_params=pltpu.CompilerParams(vmem_limit_bytes=8 << 20),
    )(*ready)
    return og.reshape(S, C, TH, W), mg.reshape(1, C, C, 2 * M1), lg


def solution(mesh):
    in_specs = (P("dp", None, "tile", None), P("dp", None, "tile", None), P("tile", None, None, None), P())
    out_specs = (P("dp", None, "tile", None), P("tile", None, None, None), P())
    return jax.shard_map(step, mesh=mesh, in_specs=in_specs, out_specs=out_specs, check_vma=False)
```

```python
import math

import jax
import jax.numpy as jnp
import numpy as np
from jax import lax
from jax.experimental import pallas as pl
from jax.experimental.pallas import tpu as pltpu
from jax.sharding import PartitionSpec as P

C = 64
M1 = 64
M2 = 64
W = 256
TH = 16
H = 1024
N_TILE = 64
N_DP = 4
S = 2
RH = 8
RL = 2
FAR_FIRST = (4, 3, 5, 2, 6, 1, 7, 0)
SPEC = 1.0 / math.sqrt(H * W)
MODE = 1.0 / math.sqrt(M1 * M2)
F32 = jnp.float32
BF16 = jnp.bfloat16
MESH = pl.DeviceIdType.MESH


def column_rows():
    phase = np.mod(np.arange(M2)[:, None] * np.arange(W)[None, :], W) * (2.0 * math.pi / W)
    return np.stack([np.cos(phase), -np.sin(phase)], axis=1).reshape(2 * M2, W)


def row_maps():
    modes = np.arange(M1)
    signed = np.where(modes < M1 // 2, modes, modes - M1)
    phase = np.mod(np.arange(H)[:, None] * signed[None, :], H) * (2.0 * math.pi / H)
    cosine = np.cos(phase).reshape(N_TILE, RH, RL, M1)
    sine = np.sin(phase).reshape(N_TILE, RH, RL, M1)
    first = np.concatenate([cosine, -sine], axis=-1)
    second = np.concatenate([sine, cosine], axis=-1)
    return np.stack([first, second], axis=1).reshape(N_TILE * 2 * RH, RL * 2 * M1)


def mm(left, right):
    return lax.dot_general(left, right, (((1,), (0,)), ((), ())), preferred_element_type=F32)


def mm_nt(left, right):
    return lax.dot_general(left, right, (((1,), (1,)), ((), ())), preferred_element_type=F32)


def gelu_slope(values):
    cumulative = 0.5 * (1.0 + lax.erf(values * (1.0 / math.sqrt(2.0))))
    density = jnp.exp(-0.5 * values * values) * (1.0 / math.sqrt(2.0 * math.pi))
    return cumulative + values * density


def input_gradient(received, grad, mix, col, b32, wide, result):
    b32[...] = received[...].astype(F32)

    def back(r, carry):
        spectral = b32[pl.ds(r, 128, stride=RH), :].T.astype(BF16)
        value = mm(spectral, col[...]) + mm(mix[...], grad[pl.ds(pl.multiple_of(r * 128, 128), 128), :])
        for n in range(RL):
            for half in range(2):
                wide[half, pl.ds(2 * r + n, C, stride=TH), :] = value[n * C:(n + 1) * C, half * 128:(half + 1) * 128]
        return carry

    lax.fori_loop(0, RH, back, 0, unroll=2)
    for half in range(2):
        result[:, half * 128:(half + 1) * 128] = wide[half].astype(BF16)


def finish(og0, mg, lg, last, ggl, mixl, coll, og_hbm, mg_hbm, lg_hbm, b32, wide, og1, sem):
    copies = [
        pltpu.make_async_copy(a, b, sem.at[n])
        for n, (a, b) in enumerate([(mg, mg_hbm), (og0, og_hbm.at[0]), (lg, lg_hbm), (og1, og_hbm.at[1])])
    ]
    for copy in copies[:3]:
        copy.start()
    input_gradient(last, ggl, mixl, coll, b32, wide, og1)
    copies[3].start()
    for copy in copies:
        copy.wait()


def kernel(v_hbm, ct_hbm, w_hbm, l_hbm, col_hbm, inv_hbm, fwd_hbm,
           og, mg, lg, last, ggl, mixl, coll,
           v, vn, v32, ctn, ct, w16, w32, wt32, l16, mix, col, inv, fwd, m32, b32, gg, snd, rcv,
           xs, ds, xall, dall, pa, pb, x1, x2, d1, d2, lga, lgs, lg1, lgr, lgp, lgd, lge, lgf,
           load_sem, send_sem, recv_sem, dp_send, dp_recv, lg_send, lg_recv):
    me = lax.axis_index("tile")
    my = lax.axis_index("dp")
    me_y, me_x, me_z = lax.div(me, 32), lax.rem(lax.div(me, 8), 4), lax.rem(me, 8)

    turn = 1 - 2 * lax.rem(me_z, 2)
    column_of = [lax.rem(me_z + turn * dz + 8, 8) for dz in range(8)]

    def plane(k):
        kx = lax.rem(k, 4)
        dx = lax.rem(1 + 2 * kx + lax.div(kx, 2), 4)
        dy = 1 - lax.div(k, 4)
        return lax.rem(me_y + dy, 2) * 32 + lax.rem(me_x + dx, 4) * 8

    def to_others(send):
        def planes(k, carry):
            base = plane(k)
            for dz in FAR_FIRST:
                send(base + column_of[dz])
            return carry

        lax.fori_loop(0, 7, planes, 0)
        for dz in FAR_FIRST[:-1]:
            send(me_y * 32 + me_x * 8 + column_of[dz])

    def group(j):
        return lax.rem(my + j, N_DP)

    loads = [
        pltpu.make_async_copy(a, b, load_sem.at[n])
        for n, (a, b) in enumerate([
            (col_hbm, col), (v_hbm.at[0], vn.at[0]), (v_hbm.at[1], vn.at[1]), (fwd_hbm, fwd),
            (w_hbm, w16), (inv_hbm, inv), (l_hbm, l16), (ct_hbm, ctn)])
    ]
    for copy in loads:
        copy.start()

    barrier = pltpu.get_barrier_semaphore()

    def greet(p):
        pl.semaphore_signal(barrier, inc=1, device_id={"tile": p}, device_id_type=MESH)

    to_others(greet)
    for j in range(1, N_DP):
        pl.semaphore_signal(barrier, inc=1, device_id={"dp": group(j)}, device_id_type=MESH)

    lane = lax.broadcasted_iota(jnp.int32, (C, 128), 1)
    low = lane < 64
    sgn = jnp.where(low, 1.0, -1.0).astype(F32)

    def exchange(phase, s):
        def send(p):
            pltpu.make_async_remote_copy(
                src_ref=snd.at[phase, s, pl.ds(pl.multiple_of(p * 16, 16), 16), :],
                dst_ref=rcv.at[phase, s, pl.ds(pl.multiple_of(me * 16, 16), 16), :],
                send_sem=send_sem.at[phase, s], recv_sem=recv_sem.at[phase, s],
                device_id={"tile": p}, device_id_type=MESH).start()

        to_others(send)
        mine = pl.ds(pl.multiple_of(me * 16, 16), 16)
        pltpu.make_async_copy(
            snd.at[phase, s, mine, :], rcv.at[phase, s, mine, :], recv_sem.at[phase, s]).start()

    def arrived(phase, s):
        pltpu.make_async_copy(rcv.at[phase, s], rcv.at[phase, s], recv_sem.at[phase, s]).wait()

    def to_group(src, dst, s, n):
        for j in range(1, N_DP):
            pltpu.make_async_remote_copy(
                src_ref=src.at[s], dst_ref=dst.at[my, s], send_sem=dp_send.at[n], recv_sem=dp_recv.at[n],
                device_id={"dp": group(j)}, device_id_type=MESH).start()
        pltpu.make_async_copy(src.at[s], dst.at[my, s], dp_recv.at[n]).start()

    def pack(phase, s):
        snd[phase, s] = m32[...].astype(BF16)

    def rows_of(natural, r):
        return jnp.concatenate([
            jnp.concatenate([natural[half, pl.ds(2 * r + n, C, stride=TH), :] for half in range(2)], axis=1)
            for n in range(RL)], axis=0)

    def widen_into(natural, source):
        for half in range(2):
            natural[half] = source[:, half * 128:(half + 1) * 128].astype(F32)

    loads[0].wait()
    for s in range(S):
        loads[1 + s].wait()

        def column(r, carry):
            tile = rows_of(v32, r).astype(BF16)
            v[s, pl.ds(pl.multiple_of(r * 128, 128), 128), :] = tile
            m32[pl.ds(r, 128, stride=RH), :] = mm_nt(col[...], tile)
            return carry

        widen_into(v32, vn.at[s])
        lax.fori_loop(0, RH, column, 0, unroll=2)
        pack(0, s)
        if s == 0:
            pl.semaphore_wait(barrier, N_TILE - 1 + N_DP - 1)
        exchange(0, s)

    loads[4].wait()

    def widen(c, carry):
        at = pl.ds(pl.multiple_of(c * 64, 64), 64)
        w32[at, :] = w16[at, :].astype(F32)
        return carry

    lax.fori_loop(0, C, widen, 0, unroll=4)
    loads[6].wait()
    mix[...] = jnp.zeros_like(mix)
    pointwise = l16[...].astype(F32)
    mix[0, :64, :64] = pointwise.T
    mix[0, 64:, 64:] = pointwise.T
    mix[1, :64, :64] = pointwise
    mix[1, 64:, 64:] = pointwise
    loads[7].wait()
    for s in range(S):
        widen_into(ct.at[s], ctn.at[s])

    def spectrum(phase, s, scale):
        both = mm(fwd[...], rcv[phase, s])
        turned = (both[:128] + pltpu.roll(both[128:], 64, 1)).T
        return (turned[:64] * scale).astype(BF16)

    def halves(value):
        wide = value.astype(F32)
        other = pltpu.roll(wide, 64, 1)
        pa[...] = jnp.where(low, wide, other)
        pb[...] = jnp.where(low, other, wide)

    def mix_rows(table):
        def step(c, carry):
            first, second = carry
            block = table[pl.ds(pl.multiple_of(c * 64, 64), 64), :]
            return first + pa[pl.ds(c, 1), :] * block, second + pb[pl.ds(c, 1), :] * block

        zero = jnp.zeros((C, 128), F32)
        return lax.fori_loop(0, C, step, (zero, zero), unroll=4)

    def back_to_rows(phase, s, value, scale):
        small = value.astype(BF16).astype(F32) * scale
        none = jnp.zeros((C, 128), F32)
        right = jnp.concatenate(
            [jnp.concatenate([small, none], axis=1), jnp.concatenate([none, small], axis=1)], axis=0).T.astype(BF16)

        def rows(n, carry):
            at = pl.ds(pl.multiple_of(n * 256, 256), 256)
            snd[phase, s, at, :] = mm(inv[at, :], right).astype(BF16)
            return carry

        lax.fori_loop(0, 4, rows, 0)

    loads[3].wait()
    loads[5].wait()
    for s in range(S):
        arrived(0, s)
        xs[s] = spectrum(0, s, SPEC)
        to_group(xs, xall, s, 0)
        halves(xs[s])
        first, second = mix_rows(w32)
        back_to_rows(1, s, first - sgn * pltpu.roll(second, 64, 1), MODE)
        exchange(1, s)

    def swap(o, carry):
        wt32[pl.ds(pl.multiple_of(o * 64, 64), 64), :] = w32[pl.ds(o, 64, stride=64), :]
        return carry

    lax.fori_loop(0, C, swap, 0)
    lga[...] = jnp.zeros_like(lga)

    def spread(c, carry):
        lg1[c] = lgs[pl.ds(c, 1), :]
        return carry

    def send_rows(src_of, dst, n):
        def send(p):
            pltpu.make_async_remote_copy(
                src_ref=src_of(p), dst_ref=dst.at[me], send_sem=lg_send.at[n], recv_sem=lg_recv.at[n],
                device_id={"tile": p}, device_id_type=MESH).start()

        to_others(send)
        pltpu.make_async_copy(src_of(me), dst.at[me], lg_recv.at[n]).start()

    for s in range(S):
        arrived(1, s)
        b32[...] = rcv[1, s].astype(F32)

        def gate(r, carry):
            at = pl.ds(pl.multiple_of(r * 128, 128), 128)
            spectral = b32[pl.ds(r, 128, stride=RH), :].T.astype(BF16)
            tile = v[s, at, :]
            pre = mm(spectral, col[...]) + mm(mix[0].astype(BF16), tile)
            grad = (rows_of(ct.at[s], r) * gelu_slope(pre)).astype(BF16)
            gg[s, at, :] = grad
            m32[pl.ds(r, 128, stride=RH), :] = mm_nt(col[...], grad)
            lga[...] += mm_nt(tile, grad)
            return carry

        lax.fori_loop(0, RH, gate, 0, unroll=2)
        pack(2, s)
        if s == S - 1:
            lgs[...] = lga[:64] + pltpu.roll(lga[64:], 64, 1)
            lax.fori_loop(0, C, spread, 0, unroll=4)
            send_rows(lambda p: lg1.at[p], lgr, 0)
        exchange(2, s)

    for s in range(S):
        arrived(2, s)
        ds[s] = spectrum(2, s, MODE)
        to_group(ds, dall, s, 1)
        halves(ds[s])
        first, second = mix_rows(wt32)
        back_to_rows(3, s, pltpu.roll(second, 64, 1) + sgn * first, SPEC)
        if s == 0:
            pltpu.make_async_copy(lgr, lgr, lg_recv.at[0]).wait()
            lgp[0] = jnp.sum(lgr[...], axis=0)
            for j in range(1, N_DP):
                pltpu.make_async_remote_copy(
                    src_ref=lgp.at[0], dst_ref=lgd.at[my], send_sem=lg_send.at[2], recv_sem=lg_recv.at[2],
                    device_id={"dp": group(j)}, device_id_type=MESH).start()
            pltpu.make_async_copy(lgp.at[0], lgd.at[my], lg_recv.at[2]).start()
        else:
            pltpu.make_async_copy(lgd, lgd, lg_recv.at[2]).wait()
            lge[0] = jnp.sum(lgd[...], axis=0)
            send_rows(lambda p: lge.at[0], lgf, 1)
        exchange(3, s)


    pltpu.make_async_copy(xall, xall, dp_recv.at[0]).wait()
    pltpu.make_async_copy(dall, dall, dp_recv.at[1]).wait()
    for g in range(N_DP):
        for s in range(S):
            n = g * S + s
            wide = xall[g, s].astype(F32)
            other = pltpu.roll(wide, 64, 1)
            x1[n] = jnp.where(low, wide, other)
            x2[n] = jnp.where(low, other, -wide)
            grad = dall[g, s].astype(F32)
            d1[n] = grad
            d2[n] = pltpu.roll(grad, 64, 1)

    def outer(c, carry):
        even = jnp.zeros((C, 128), F32)
        odd = jnp.zeros((C, 128), F32)
        for n in range(N_DP * S):
            first, second = d1[n], d2[n]
            even += x1[n, pl.ds(2 * c, 1), :] * first + x2[n, pl.ds(2 * c, 1), :] * second
            odd += x1[n, pl.ds(2 * c + 1, 1), :] * first + x2[n, pl.ds(2 * c + 1, 1), :] * second
        at = pl.multiple_of(c * 128, 128)
        mg[pl.ds(at, 64), :] = even
        mg[pl.ds(at + 64, 64), :] = odd
        return carry

    lax.fori_loop(0, C // 2, outer, 0)

    mixl[...] = mix[1].astype(BF16)
    coll[...] = col[...]
    ggl[...] = gg[1]
    arrived(3, 0)
    input_gradient(rcv.at[3, 0], gg.at[0], mixl, col, b32, v32, og)

    pltpu.make_async_copy(lgf, lgf, lg_recv.at[1]).wait()

    def gather(c, carry):
        lgs[pl.ds(c, 1), :] = lgf[c]
        return carry

    lax.fori_loop(0, C, gather, 0)
    lg[...] = lgs[:, :C]
    arrived(3, 1)
    last[...] = rcv[3, 1]

    for phase in range(4):
        for s in range(S):
            sent = snd.at[phase, s, pl.ds(0, 16 * (N_TILE - 1)), :]
            pltpu.make_async_copy(sent, sent, send_sem.at[phase, s]).wait()
    for n, ref in ((0, xall), (1, dall)):
        sent = ref.at[pl.ds(0, N_DP - 1)]
        pltpu.make_async_copy(sent, sent, dp_send.at[n]).wait()
    for n in range(2):
        sent = lgr.at[pl.ds(0, N_TILE - 1)]
        pltpu.make_async_copy(sent, sent, lg_send.at[n]).wait()
    sent = lgd.at[pl.ds(0, N_DP - 1)]
    pltpu.make_async_copy(sent, sent, lg_send.at[2]).wait()


def step(inputs, cotangent, mode_weight, local_weight):
    rows = row_maps()
    col = jnp.asarray(column_rows(), BF16)
    inv = jnp.asarray(rows, BF16)
    fwd = jnp.asarray(np.ascontiguousarray(rows.T), BF16)
    dma = pltpu.SemaphoreType.DMA
    vm = pltpu.VMEM
    here = pl.BlockSpec(memory_space=pltpu.VMEM)
    anywhere = pl.BlockSpec(memory_space=pl.ANY)
    ready = pl.pallas_call(
        kernel,
        out_shape=(
            jax.ShapeDtypeStruct((C * TH, W), BF16),
            jax.ShapeDtypeStruct((C * C, 2 * M1), F32),
            jax.ShapeDtypeStruct((C, C), F32),
            jax.ShapeDtypeStruct((1024, 128), BF16),
            jax.ShapeDtypeStruct((TH * C, W), BF16),
            jax.ShapeDtypeStruct((128, 128), BF16),
            jax.ShapeDtypeStruct((128, W), BF16),
        ),
        in_specs=[anywhere] * 7,
        out_specs=(here,) * 7,
        scratch_shapes=[
            vm((S, TH * C, W), BF16), vm((S, TH * C, W), BF16), vm((2, TH * C, 128), F32),
            vm((S, TH * C, W), BF16), vm((S, 2, TH * C, 128), F32),
            vm((C * C, 128), BF16), vm((C * C, 128), F32), vm((C * C, 128), F32),
            vm((C, C), BF16), vm((2, 128, 128), F32), vm((128, W), BF16), vm((1024, 256), BF16), vm((256, 1024), BF16),
            vm((1024, 128), F32), vm((1024, 128), F32),
            vm((S, TH * C, W), BF16),
            vm((4, S, 1024, 128), BF16), vm((4, S, 1024, 128), BF16),
            vm((S, C, 128), BF16), vm((S, C, 128), BF16),
            vm((N_DP, S, C, 128), BF16), vm((N_DP, S, C, 128), BF16),
            vm((C, 128), F32), vm((C, 128), F32),
            vm((N_DP * S, C, 128), F32), vm((N_DP * S, C, 128), F32),
            vm((N_DP * S, C, 128), F32), vm((N_DP * S, C, 128), F32),
            vm((128, 128), F32), vm((C, 128), F32),
            vm((C, 1, 128), F32), vm((C, 1, 128), F32), vm((1, 1, 128), F32), vm((N_DP, 1, 128), F32),
            vm((1, 1, 128), F32), vm((C, 1, 128), F32),
            dma((8,)), dma((4, S)), dma((4, S)), dma((2,)), dma((2,)), dma((3,)), dma((3,)),
        ],
        compiler_params=pltpu.CompilerParams(
            collective_id=0, has_side_effects=True, vmem_limit_bytes=40 << 20),
    )(*[pltpu.with_memory_space_constraint(a, pltpu.HBM) for a in (
        inputs.reshape(S, C * TH, W), cotangent.reshape(S, C * TH, W), mode_weight.reshape(C * C, 2 * M1),
        local_weight, col, inv, fwd)])
    og, mg, lg = pl.pallas_call(
        finish,
        out_shape=(
            jax.ShapeDtypeStruct((S, C * TH, W), BF16),
            jax.ShapeDtypeStruct((C * C, 2 * M1), F32),
            jax.ShapeDtypeStruct((C, C), F32),
        ),
        in_specs=[anywhere, anywhere, anywhere, here, here, here, here],
        out_specs=(anywhere,) * 3,
        scratch_shapes=[vm((1024, 128), F32), vm((2, TH * C, 128), F32), vm((C * TH, W), BF16), dma((4,))],
        compiler_params=pltpu.CompilerParams(vmem_limit_bytes=8 << 20),
    )(*ready)
    return og.reshape(S, C, TH, W), mg.reshape(1, C, C, 2 * M1), lg


def solution(mesh):
    in_specs = (P("dp", None, "tile", None), P("dp", None, "tile", None), P("tile", None, None, None), P())
    out_specs = (P("dp", None, "tile", None), P("tile", None, None, None), P())
    return jax.shard_map(step, mesh=mesh, in_specs=in_specs, out_specs=out_specs, check_vma=False)
```

```python
import math

import jax
import jax.numpy as jnp
import numpy as np
from jax import lax
from jax.experimental import pallas as pl
from jax.experimental.pallas import tpu as pltpu
from jax.sharding import PartitionSpec as P

C = 64
M1 = 64
M2 = 64
W = 256
TH = 16
H = 1024
N_TILE = 64
N_DP = 4
S = 2
RH = 8
RL = 2
FAR_FIRST = (4, 3, 5, 2, 6, 1, 7, 0)
SPEC = 1.0 / math.sqrt(H * W)
MODE = 1.0 / math.sqrt(M1 * M2)
F32 = jnp.float32
BF16 = jnp.bfloat16
MESH = pl.DeviceIdType.MESH


def column_rows():
    phase = np.mod(np.arange(M2)[:, None] * np.arange(W)[None, :], W) * (2.0 * math.pi / W)
    return np.stack([np.cos(phase), -np.sin(phase)], axis=1).reshape(2 * M2, W)


def row_maps():
    modes = np.arange(M1)
    signed = np.where(modes < M1 // 2, modes, modes - M1)
    phase = np.mod(np.arange(H)[:, None] * signed[None, :], H) * (2.0 * math.pi / H)
    cosine = np.cos(phase).reshape(N_TILE, RH, RL, M1)
    sine = np.sin(phase).reshape(N_TILE, RH, RL, M1)
    first = np.concatenate([cosine, -sine], axis=-1)
    second = np.concatenate([sine, cosine], axis=-1)
    return np.stack([first, second], axis=1).reshape(N_TILE * 2 * RH, RL * 2 * M1)


def mm(left, right):
    return lax.dot_general(left, right, (((1,), (0,)), ((), ())), preferred_element_type=F32)


def mm_nt(left, right):
    return lax.dot_general(left, right, (((1,), (1,)), ((), ())), preferred_element_type=F32)


def gelu_slope(values):
    cumulative = 0.5 * (1.0 + lax.erf(values * (1.0 / math.sqrt(2.0))))
    density = jnp.exp(-0.5 * values * values) * (1.0 / math.sqrt(2.0 * math.pi))
    return cumulative + values * density


def input_gradient(received, grad, mix, col, b32, wide, result):
    b32[...] = received[...].astype(F32)

    def back(r, carry):
        spectral = b32[pl.ds(r, 128, stride=RH), :].T.astype(BF16)
        value = mm(spectral, col[...]) + mm(mix[...], grad[pl.ds(pl.multiple_of(r * 128, 128), 128), :])
        for n in range(RL):
            for half in range(2):
                wide[half, pl.ds(2 * r + n, C, stride=TH), :] = value[n * C:(n + 1) * C, half * 128:(half + 1) * 128]
        return carry

    lax.fori_loop(0, RH, back, 0, unroll=4)
    for half in range(2):
        result[:, half * 128:(half + 1) * 128] = wide[half].astype(BF16)


def finish(og0, mg, lg, last, ggl, mixl, coll, og_hbm, mg_hbm, lg_hbm, b32, wide, og1, sem):
    copies = [
        pltpu.make_async_copy(a, b, sem.at[n])
        for n, (a, b) in enumerate([(mg, mg_hbm), (og0, og_hbm.at[0]), (lg, lg_hbm), (og1, og_hbm.at[1])])
    ]
    for copy in copies[:3]:
        copy.start()
    input_gradient(last, ggl, mixl, coll, b32, wide, og1)
    copies[3].start()
    for copy in copies:
        copy.wait()


def kernel(v_hbm, ct_hbm, w_hbm, l_hbm, col_hbm, inv_hbm, fwd_hbm,
           og, mg, lg, last, ggl, mixl, coll,
           v, vn, v32, ctn, ct, w16, w32, wt32, l16, mix, col, inv, fwd, m32, b32, gg, snd, rcv,
           xs, ds, xall, dall, pa, pb, x1, x2, d1, d2, lga, lgs, lgd, lgp, lgr, lge, lgz, lgq, lgf,
           load_sem, send_sem, recv_sem, dp_send, dp_recv, lg_send, lg_recv):
    me = lax.axis_index("tile")
    my = lax.axis_index("dp")
    me_y, me_x, me_z = lax.div(me, 32), lax.rem(lax.div(me, 8), 4), lax.rem(me, 8)

    turn = 1 - 2 * lax.rem(me_z, 2)
    column_of = [lax.rem(me_z + turn * dz + 8, 8) for dz in range(8)]

    def plane(k):
        kx = lax.rem(k, 4)
        dx = lax.rem(1 + 2 * kx + lax.div(kx, 2), 4)
        dy = 1 - lax.div(k, 4)
        return lax.rem(me_y + dy, 2) * 32 + lax.rem(me_x + dx, 4) * 8

    def to_others(send):
        def planes(k, carry):
            base = plane(k)
            for dz in FAR_FIRST:
                send(base + column_of[dz])
            return carry

        lax.fori_loop(0, 7, planes, 0)
        for dz in FAR_FIRST[:-1]:
            send(me_y * 32 + me_x * 8 + column_of[dz])

    def group(j):
        return lax.rem(my + j, N_DP)

    loads = [
        pltpu.make_async_copy(a, b, load_sem.at[n])
        for n, (a, b) in enumerate([
            (col_hbm, col), (v_hbm.at[0], vn.at[0]), (v_hbm.at[1], vn.at[1]), (fwd_hbm, fwd),
            (w_hbm, w16), (inv_hbm, inv), (l_hbm, l16), (ct_hbm, ctn)])
    ]
    for copy in loads:
        copy.start()

    barrier = pltpu.get_barrier_semaphore()

    def greet(p):
        pl.semaphore_signal(barrier, inc=1, device_id={"tile": p}, device_id_type=MESH)

    to_others(greet)
    for j in range(1, N_DP):
        pl.semaphore_signal(barrier, inc=1, device_id={"dp": group(j)}, device_id_type=MESH)

    lane = lax.broadcasted_iota(jnp.int32, (C, 128), 1)
    low = lane < 64
    sgn = jnp.where(low, 1.0, -1.0).astype(F32)

    def exchange(phase, s):
        def send(p):
            pltpu.make_async_remote_copy(
                src_ref=snd.at[phase, s, pl.ds(pl.multiple_of(p * 16, 16), 16), :],
                dst_ref=rcv.at[phase, s, pl.ds(pl.multiple_of(me * 16, 16), 16), :],
                send_sem=send_sem.at[phase, s], recv_sem=recv_sem.at[phase, s],
                device_id={"tile": p}, device_id_type=MESH).start()

        to_others(send)
        mine = pl.ds(pl.multiple_of(me * 16, 16), 16)
        pltpu.make_async_copy(
            snd.at[phase, s, mine, :], rcv.at[phase, s, mine, :], recv_sem.at[phase, s]).start()

    def arrived(phase, s):
        pltpu.make_async_copy(rcv.at[phase, s], rcv.at[phase, s], recv_sem.at[phase, s]).wait()

    def to_group(src, dst, s, n):
        for j in range(1, N_DP):
            pltpu.make_async_remote_copy(
                src_ref=src.at[s], dst_ref=dst.at[my, s], send_sem=dp_send.at[n], recv_sem=dp_recv.at[n],
                device_id={"dp": group(j)}, device_id_type=MESH).start()
        pltpu.make_async_copy(src.at[s], dst.at[my, s], dp_recv.at[n]).start()

    def pack(phase, s):
        snd[phase, s] = m32[...].astype(BF16)

    def rows_of(natural, r):
        return jnp.concatenate([
            jnp.concatenate([natural[half, pl.ds(2 * r + n, C, stride=TH), :] for half in range(2)], axis=1)
            for n in range(RL)], axis=0)

    def widen_into(natural, source):
        for half in range(2):
            natural[half] = source[:, half * 128:(half + 1) * 128].astype(F32)

    loads[0].wait()
    for s in range(S):
        loads[1 + s].wait()

        def column(r, carry):
            tile = rows_of(v32, r).astype(BF16)
            v[s, pl.ds(pl.multiple_of(r * 128, 128), 128), :] = tile
            m32[pl.ds(r, 128, stride=RH), :] = mm_nt(col[...], tile)
            return carry

        widen_into(v32, vn.at[s])
        lax.fori_loop(0, RH, column, 0, unroll=4)
        pack(0, s)
        if s == 0:
            pl.semaphore_wait(barrier, N_TILE - 1 + N_DP - 1)
        exchange(0, s)

    loads[4].wait()

    def widen(c, carry):
        at = pl.ds(pl.multiple_of(c * 64, 64), 64)
        w32[at, :] = w16[at, :].astype(F32)
        return carry

    lax.fori_loop(0, C, widen, 0, unroll=4)
    loads[6].wait()
    mix[...] = jnp.zeros_like(mix)
    pointwise = l16[...].astype(F32)
    mix[0, :64, :64] = pointwise.T
    mix[0, 64:, 64:] = pointwise.T
    mix[1, :64, :64] = pointwise
    mix[1, 64:, 64:] = pointwise
    loads[7].wait()
    for s in range(S):
        widen_into(ct.at[s], ctn.at[s])

    def spectrum(phase, s, scale):
        both = mm(fwd[...], rcv[phase, s])
        turned = (both[:128] + pltpu.roll(both[128:], 64, 1)).T
        return (turned[:64] * scale).astype(BF16)

    def halves(value):
        wide = value.astype(F32)
        other = pltpu.roll(wide, 64, 1)
        pa[...] = jnp.where(low, wide, other)
        pb[...] = jnp.where(low, other, wide)

    def mix_rows(table):
        def step(c, carry):
            first, second = carry
            block = table[pl.ds(pl.multiple_of(c * 64, 64), 64), :]
            return first + pa[pl.ds(c, 1), :] * block, second + pb[pl.ds(c, 1), :] * block

        zero = jnp.zeros((C, 128), F32)
        return lax.fori_loop(0, C, step, (zero, zero), unroll=8)

    def back_to_rows(phase, s, value, scale):
        small = value.astype(BF16).astype(F32) * scale
        none = jnp.zeros((C, 128), F32)
        right = jnp.concatenate(
            [jnp.concatenate([small, none], axis=1), jnp.concatenate([none, small], axis=1)], axis=0).T.astype(BF16)

        def rows(n, carry):
            at = pl.ds(pl.multiple_of(n * 256, 256), 256)
            snd[phase, s, at, :] = mm(inv[at, :], right).astype(BF16)
            return carry

        lax.fori_loop(0, 4, rows, 0, unroll=4)

    loads[3].wait()
    loads[5].wait()
    for s in range(S):
        arrived(0, s)
        xs[s] = spectrum(0, s, SPEC)
        halves(xs[s])
        first, second = mix_rows(w32)
        back_to_rows(1, s, first - sgn * pltpu.roll(second, 64, 1), MODE)
        exchange(1, s)
        to_group(xs, xall, s, 0)

    def swap(o, carry):
        wt32[pl.ds(pl.multiple_of(o * 64, 64), 64), :] = w32[pl.ds(o, 64, stride=64), :]
        return carry

    lax.fori_loop(0, C, swap, 0)
    lga[...] = jnp.zeros_like(lga)

    my_plane = lax.div(me, 8)

    def to_plane(src_of, dst, n):
        for k in range(1, 8):
            other = lax.rem(me_y + k // 4, 2) * 4 + lax.rem(me_x + k % 4, 4)
            pltpu.make_async_remote_copy(
                src_ref=src_of(other), dst_ref=dst.at[my_plane], send_sem=lg_send.at[n], recv_sem=lg_recv.at[n],
                device_id={"tile": other * 8 + me_z}, device_id_type=MESH).start()
        pltpu.make_async_copy(src_of(my_plane), dst.at[my_plane], lg_recv.at[n]).start()

    def collected(ref, n):
        pltpu.make_async_copy(ref, ref, lg_recv.at[n]).wait()

    def point_hop(n):
        if n == 0:
            lgs[...] = lga[:64] + pltpu.roll(lga[64:], 64, 1)
            for j in range(1, N_DP):
                pltpu.make_async_remote_copy(
                    src_ref=lgs, dst_ref=lgd.at[my], send_sem=lg_send.at[0], recv_sem=lg_recv.at[0],
                    device_id={"dp": group(j)}, device_id_type=MESH).start()
            pltpu.make_async_copy(lgs, lgd.at[my], lg_recv.at[0]).start()
        elif n == 1:
            collected(lgd, 0)
            lgp[...] = jnp.sum(lgd[...], axis=0).reshape(8, 8, 128)
            to_plane(lambda other: lgp.at[other], lgr, 1)
        elif n == 2:
            collected(lgr, 1)
            lge[...] = jnp.sum(lgr[...], axis=0)
            for dz in range(1, 8):
                z = lax.rem(me_z + dz, 8)
                pltpu.make_async_remote_copy(
                    src_ref=lge, dst_ref=lgz.at[me_z], send_sem=lg_send.at[2], recv_sem=lg_recv.at[2],
                    device_id={"tile": me - me_z + z}, device_id_type=MESH).start()
            pltpu.make_async_copy(lge, lgz.at[me_z], lg_recv.at[2]).start()
        elif n == 3:
            collected(lgz, 2)
            lgq[...] = jnp.sum(lgz[...], axis=0)
            to_plane(lambda other: lgq, lgf, 3)
        else:
            collected(lgf, 3)
            lg[...] = lgf[...].reshape(C, 128)[:, :C]

    for s in range(S):
        arrived(1, s)
        b32[...] = rcv[1, s].astype(F32)

        def gate(r, carry):
            at = pl.ds(pl.multiple_of(r * 128, 128), 128)
            spectral = b32[pl.ds(r, 128, stride=RH), :].T.astype(BF16)
            tile = v[s, at, :]
            pre = mm(spectral, col[...]) + mm(mix[0].astype(BF16), tile)
            grad = (rows_of(ct.at[s], r) * gelu_slope(pre)).astype(BF16)
            gg[s, at, :] = grad
            m32[pl.ds(r, 128, stride=RH), :] = mm_nt(col[...], grad)
            lga[...] += mm_nt(tile, grad)
            return carry

        lax.fori_loop(0, RH, gate, 0, unroll=4)
        pack(2, s)
        if s == S - 1:
            point_hop(0)
        exchange(2, s)

    for s in range(S):
        arrived(2, s)
        ds[s] = spectrum(2, s, MODE)
        to_group(ds, dall, s, 1)
        halves(ds[s])
        first, second = mix_rows(wt32)
        back_to_rows(3, s, pltpu.roll(second, 64, 1) + sgn * first, SPEC)
        point_hop(1 + s)
        exchange(3, s)


    pltpu.make_async_copy(xall, xall, dp_recv.at[0]).wait()
    pltpu.make_async_copy(dall, dall, dp_recv.at[1]).wait()
    for g in range(N_DP):
        for s in range(S):
            n = g * S + s
            wide = xall[g, s].astype(F32)
            other = pltpu.roll(wide, 64, 1)
            x1[n] = jnp.where(low, wide, other)
            x2[n] = jnp.where(low, other, -wide)
            grad = dall[g, s].astype(F32)
            d1[n] = grad
            d2[n] = pltpu.roll(grad, 64, 1)

    def outer(c, carry):
        even = jnp.zeros((C, 128), F32)
        odd = jnp.zeros((C, 128), F32)
        for n in range(N_DP * S):
            first, second = d1[n], d2[n]
            even += x1[n, pl.ds(2 * c, 1), :] * first + x2[n, pl.ds(2 * c, 1), :] * second
            odd += x1[n, pl.ds(2 * c + 1, 1), :] * first + x2[n, pl.ds(2 * c + 1, 1), :] * second
        at = pl.multiple_of(c * 128, 128)
        mg[pl.ds(at, 64), :] = even
        mg[pl.ds(at + 64, 64), :] = odd
        return carry

    lax.fori_loop(0, C // 2, outer, 0)
    point_hop(3)

    mixl[...] = mix[1].astype(BF16)
    coll[...] = col[...]
    ggl[...] = gg[1]
    arrived(3, 0)
    input_gradient(rcv.at[3, 0], gg.at[0], mixl, col, b32, v32, og)

    point_hop(4)
    arrived(3, 1)
    last[...] = rcv[3, 1]

    for phase in range(4):
        for s in range(S):
            sent = snd.at[phase, s, pl.ds(0, 16 * (N_TILE - 1)), :]
            pltpu.make_async_copy(sent, sent, send_sem.at[phase, s]).wait()
    for n, ref in ((0, xall), (1, dall)):
        sent = ref.at[pl.ds(0, N_DP - 1)]
        pltpu.make_async_copy(sent, sent, dp_send.at[n]).wait()
    for n, ref, count in ((0, lgd, N_DP), (1, lgr, 8), (2, lgz, 8), (3, lgf, 8)):
        sent = ref.at[pl.ds(0, count - 1)]
        pltpu.make_async_copy(sent, sent, lg_send.at[n]).wait()


def step(inputs, cotangent, mode_weight, local_weight):
    rows = row_maps()
    col = jnp.asarray(column_rows(), BF16)
    inv = jnp.asarray(rows, BF16)
    fwd = jnp.asarray(np.ascontiguousarray(rows.T), BF16)
    dma = pltpu.SemaphoreType.DMA
    vm = pltpu.VMEM
    here = pl.BlockSpec(memory_space=pltpu.VMEM)
    anywhere = pl.BlockSpec(memory_space=pl.ANY)
    ready = pl.pallas_call(
        kernel,
        out_shape=(
            jax.ShapeDtypeStruct((C * TH, W), BF16),
            jax.ShapeDtypeStruct((C * C, 2 * M1), F32),
            jax.ShapeDtypeStruct((C, C), F32),
            jax.ShapeDtypeStruct((1024, 128), BF16),
            jax.ShapeDtypeStruct((TH * C, W), BF16),
            jax.ShapeDtypeStruct((128, 128), BF16),
            jax.ShapeDtypeStruct((128, W), BF16),
        ),
        in_specs=[anywhere] * 7,
        out_specs=(here,) * 7,
        scratch_shapes=[
            vm((S, TH * C, W), BF16), vm((S, TH * C, W), BF16), vm((2, TH * C, 128), F32),
            vm((S, TH * C, W), BF16), vm((S, 2, TH * C, 128), F32),
            vm((C * C, 128), BF16), vm((C * C, 128), F32), vm((C * C, 128), F32),
            vm((C, C), BF16), vm((2, 128, 128), F32), vm((128, W), BF16), vm((1024, 256), BF16), vm((256, 1024), BF16),
            vm((1024, 128), F32), vm((1024, 128), F32),
            vm((S, TH * C, W), BF16),
            vm((4, S, 1024, 128), BF16), vm((4, S, 1024, 128), BF16),
            vm((S, C, 128), BF16), vm((S, C, 128), BF16),
            vm((N_DP, S, C, 128), BF16), vm((N_DP, S, C, 128), BF16),
            vm((C, 128), F32), vm((C, 128), F32),
            vm((N_DP * S, C, 128), F32), vm((N_DP * S, C, 128), F32),
            vm((N_DP * S, C, 128), F32), vm((N_DP * S, C, 128), F32),
            vm((128, 128), F32), vm((C, 128), F32),
            vm((N_DP, C, 128), F32), vm((8, 8, 128), F32), vm((8, 8, 128), F32),
            vm((8, 128), F32), vm((8, 8, 128), F32), vm((8, 128), F32), vm((8, 8, 128), F32),
            dma((8,)), dma((4, S)), dma((4, S)), dma((2,)), dma((2,)), dma((4,)), dma((4,)),
        ],
        compiler_params=pltpu.CompilerParams(
            collective_id=0, has_side_effects=True, vmem_limit_bytes=40 << 20),
    )(*[pltpu.with_memory_space_constraint(a, pltpu.HBM) for a in (
        inputs.reshape(S, C * TH, W), cotangent.reshape(S, C * TH, W), mode_weight.reshape(C * C, 2 * M1),
        local_weight, col, inv, fwd)])
    og, mg, lg = pl.pallas_call(
        finish,
        out_shape=(
            jax.ShapeDtypeStruct((S, C * TH, W), BF16),
            jax.ShapeDtypeStruct((C * C, 2 * M1), F32),
            jax.ShapeDtypeStruct((C, C), F32),
        ),
        in_specs=[anywhere, anywhere, anywhere, here, here, here, here],
        out_specs=(anywhere,) * 3,
        scratch_shapes=[vm((1024, 128), F32), vm((2, TH * C, 128), F32), vm((C * TH, W), BF16), dma((4,))],
        compiler_params=pltpu.CompilerParams(vmem_limit_bytes=8 << 20),
    )(*ready)
    return og.reshape(S, C, TH, W), mg.reshape(1, C, C, 2 * M1), lg


def solution(mesh):
    in_specs = (P("dp", None, "tile", None), P("dp", None, "tile", None), P("tile", None, None, None), P())
    out_specs = (P("dp", None, "tile", None), P("tile", None, None, None), P())
    return jax.shard_map(step, mesh=mesh, in_specs=in_specs, out_specs=out_specs, check_vma=False)
```

```python
import math

import jax
import jax.numpy as jnp
import numpy as np
from jax import lax
from jax.experimental import pallas as pl
from jax.experimental.pallas import tpu as pltpu
from jax.sharding import PartitionSpec as P

C = 64
M1 = 64
M2 = 64
W = 256
TH = 16
H = 1024
N_TILE = 64
N_DP = 4
S = 2
RH = 8
RL = 2
FAR_FIRST = (4, 3, 5, 2, 6, 1, 7, 0)
SPEC = 1.0 / math.sqrt(H * W)
MODE = 1.0 / math.sqrt(M1 * M2)
F32 = jnp.float32
BF16 = jnp.bfloat16
MESH = pl.DeviceIdType.MESH


def column_rows():
    phase = np.mod(np.arange(M2)[:, None] * np.arange(W)[None, :], W) * (2.0 * math.pi / W)
    return np.stack([np.cos(phase), -np.sin(phase)], axis=1).reshape(2 * M2, W)


def row_maps():
    modes = np.arange(M1)
    signed = np.where(modes < M1 // 2, modes, modes - M1)
    phase = np.mod(np.arange(H)[:, None] * signed[None, :], H) * (2.0 * math.pi / H)
    cosine = np.cos(phase).reshape(N_TILE, RH, RL, M1)
    sine = np.sin(phase).reshape(N_TILE, RH, RL, M1)
    first = np.concatenate([cosine, -sine], axis=-1)
    second = np.concatenate([sine, cosine], axis=-1)
    return np.stack([first, second], axis=1).reshape(N_TILE * 2 * RH, RL * 2 * M1)


def mm(left, right):
    return lax.dot_general(left, right, (((1,), (0,)), ((), ())), preferred_element_type=F32)


def mm_nt(left, right):
    return lax.dot_general(left, right, (((1,), (1,)), ((), ())), preferred_element_type=F32)


def gelu_slope(values):
    cumulative = 0.5 * (1.0 + lax.erf(values * (1.0 / math.sqrt(2.0))))
    density = jnp.exp(-0.5 * values * values) * (1.0 / math.sqrt(2.0 * math.pi))
    return cumulative + values * density


def pointwise_part(grad, mix, wide):
    def part(r, carry):
        value = mm(mix[...], grad[pl.ds(pl.multiple_of(r * 128, 128), 128), :])
        for n in range(RL):
            for half in range(2):
                wide[half, pl.ds(2 * r + n, C, stride=TH), :] = value[n * C:(n + 1) * C, half * 128:(half + 1) * 128]
        return carry

    lax.fori_loop(0, RH, part, 0, unroll=4)


def input_gradient(received, wide, col, b32, t32, result, done):
    b32[...] = received[...].astype(F32)

    def turn(r, carry):
        value = b32[pl.ds(r, 128, stride=RH), :].T
        for n in range(RL):
            t32[pl.ds(2 * r + n, C, stride=TH), :] = value[n * C:(n + 1) * C]
        return carry

    lax.fori_loop(0, RH, turn, 0, unroll=4)
    for n in range(4):
        at = slice(n * 256, (n + 1) * 256)
        value = mm(t32[at, :].astype(BF16), col[...])
        for half in range(2):
            lanes = slice(half * 128, (half + 1) * 128)
            result[at, lanes] = (value[:, lanes] + wide[half, at, :]).astype(BF16)
        done(n)


def finish(og0, mg, lg, last, wide, coll, og_hbm, mg_hbm, lg_hbm, b32, t32, og1, sem):
    copies = [
        pltpu.make_async_copy(a, b, sem.at[n])
        for n, (a, b) in enumerate([(mg, mg_hbm), (og0, og_hbm.at[0]), (lg, lg_hbm)] + [
            (og1.at[pl.ds(256 * n, 256), :], og_hbm.at[1, pl.ds(256 * n, 256), :]) for n in range(4)])
    ]
    for copy in copies[:3]:
        copy.start()
    input_gradient(last, wide, coll, b32, t32, og1, lambda n: copies[3 + n].start())
    for copy in copies:
        copy.wait()


def kernel(v_hbm, ct_hbm, w_hbm, l_hbm, col_hbm, inv_hbm, fwd_hbm,
           og, mg, lg, last, wide1, coll,
           v, vn, v32, ctn, ct, w16, w32, wt32, l16, mix, col, inv, fwd, m32, b32, t32, mixl, gg, snd, rcv,
           xs, ds, xall, dall, pa, pb, x1, x2, d1, d2, lga, lgs, lgd, lgp, lgr, lge, lgz, lgq, lgf,
           load_sem, send_sem, recv_sem, dp_send, dp_recv, lg_send, lg_recv):
    me = lax.axis_index("tile")
    my = lax.axis_index("dp")
    me_y, me_x, me_z = lax.div(me, 32), lax.rem(lax.div(me, 8), 4), lax.rem(me, 8)

    turn = 1 - 2 * lax.rem(me_z, 2)
    column_of = [lax.rem(me_z + turn * dz + 8, 8) for dz in range(8)]

    def plane(k):
        kx = lax.rem(k, 4)
        dx = lax.rem(1 + 2 * kx + lax.div(kx, 2), 4)
        dy = 1 - lax.div(k, 4)
        return lax.rem(me_y + dy, 2) * 32 + lax.rem(me_x + dx, 4) * 8

    def to_others(send):
        def planes(k, carry):
            base = plane(k)
            for dz in FAR_FIRST:
                send(base + column_of[dz])
            return carry

        lax.fori_loop(0, 7, planes, 0)
        for dz in FAR_FIRST[:-1]:
            send(me_y * 32 + me_x * 8 + column_of[dz])

    def group(j):
        return lax.rem(my + j, N_DP)

    loads = [
        pltpu.make_async_copy(a, b, load_sem.at[n])
        for n, (a, b) in enumerate([
            (col_hbm, col), (v_hbm.at[0], vn.at[0]), (v_hbm.at[1], vn.at[1]), (fwd_hbm, fwd),
            (w_hbm, w16), (inv_hbm, inv), (l_hbm, l16), (ct_hbm, ctn)])
    ]
    for copy in loads:
        copy.start()

    barrier = pltpu.get_barrier_semaphore()

    def greet(p):
        pl.semaphore_signal(barrier, inc=1, device_id={"tile": p}, device_id_type=MESH)

    to_others(greet)
    for j in range(1, N_DP):
        pl.semaphore_signal(barrier, inc=1, device_id={"dp": group(j)}, device_id_type=MESH)

    lane = lax.broadcasted_iota(jnp.int32, (C, 128), 1)
    low = lane < 64
    sgn = jnp.where(low, 1.0, -1.0).astype(F32)

    def exchange(phase, s):
        def send(p):
            pltpu.make_async_remote_copy(
                src_ref=snd.at[phase, s, pl.ds(pl.multiple_of(p * 16, 16), 16), :],
                dst_ref=rcv.at[phase, s, pl.ds(pl.multiple_of(me * 16, 16), 16), :],
                send_sem=send_sem.at[phase, s], recv_sem=recv_sem.at[phase, s],
                device_id={"tile": p}, device_id_type=MESH).start()

        to_others(send)
        mine = pl.ds(pl.multiple_of(me * 16, 16), 16)
        pltpu.make_async_copy(
            snd.at[phase, s, mine, :], rcv.at[phase, s, mine, :], recv_sem.at[phase, s]).start()

    def arrived(phase, s):
        pltpu.make_async_copy(rcv.at[phase, s], rcv.at[phase, s], recv_sem.at[phase, s]).wait()

    def to_group(src, dst, s, n):
        for j in range(1, N_DP):
            pltpu.make_async_remote_copy(
                src_ref=src.at[s], dst_ref=dst.at[my, s], send_sem=dp_send.at[n], recv_sem=dp_recv.at[n],
                device_id={"dp": group(j)}, device_id_type=MESH).start()
        pltpu.make_async_copy(src.at[s], dst.at[my, s], dp_recv.at[n]).start()

    def pack(phase, s):
        snd[phase, s] = m32[...].astype(BF16)

    def rows_of(natural, r):
        return jnp.concatenate([
            jnp.concatenate([natural[half, pl.ds(2 * r + n, C, stride=TH), :] for half in range(2)], axis=1)
            for n in range(RL)], axis=0)

    def widen_into(natural, source):
        for half in range(2):
            natural[half] = source[:, half * 128:(half + 1) * 128].astype(F32)

    loads[0].wait()
    for s in range(S):
        loads[1 + s].wait()

        def column(r, carry):
            tile = rows_of(v32, r).astype(BF16)
            v[s, pl.ds(pl.multiple_of(r * 128, 128), 128), :] = tile
            m32[pl.ds(r, 128, stride=RH), :] = mm_nt(col[...], tile)
            return carry

        widen_into(v32, vn.at[s])
        lax.fori_loop(0, RH, column, 0, unroll=4)
        pack(0, s)
        if s == 0:
            pl.semaphore_wait(barrier, N_TILE - 1 + N_DP - 1)
        exchange(0, s)

    loads[4].wait()

    def widen(c, carry):
        at = pl.ds(pl.multiple_of(c * 64, 64), 64)
        w32[at, :] = w16[at, :].astype(F32)
        return carry

    lax.fori_loop(0, C, widen, 0, unroll=4)
    loads[6].wait()
    mix[...] = jnp.zeros_like(mix)
    pointwise = l16[...].astype(F32)
    mix[0, :64, :64] = pointwise.T
    mix[0, 64:, 64:] = pointwise.T
    mix[1, :64, :64] = pointwise
    mix[1, 64:, 64:] = pointwise
    loads[7].wait()
    for s in range(S):
        widen_into(ct.at[s], ctn.at[s])

    def spectrum(phase, s, scale):
        both = mm(fwd[...], rcv[phase, s])
        turned = (both[:128] + pltpu.roll(both[128:], 64, 1)).T
        return (turned[:64] * scale).astype(BF16)

    def halves(value):
        wide = value.astype(F32)
        other = pltpu.roll(wide, 64, 1)
        pa[...] = jnp.where(low, wide, other)
        pb[...] = jnp.where(low, other, wide)

    def mix_rows(table):
        def step(c, carry):
            first, second = carry
            block = table[pl.ds(pl.multiple_of(c * 64, 64), 64), :]
            return first + pa[pl.ds(c, 1), :] * block, second + pb[pl.ds(c, 1), :] * block

        zero = jnp.zeros((C, 128), F32)
        return lax.fori_loop(0, C, step, (zero, zero), unroll=8)

    def back_to_rows(phase, s, value, scale):
        small = value.astype(BF16).astype(F32) * scale
        none = jnp.zeros((C, 128), F32)
        right = jnp.concatenate(
            [jnp.concatenate([small, none], axis=1), jnp.concatenate([none, small], axis=1)], axis=0).T.astype(BF16)

        def rows(n, carry):
            at = pl.ds(pl.multiple_of(n * 256, 256), 256)
            snd[phase, s, at, :] = mm(inv[at, :], right).astype(BF16)
            return carry

        lax.fori_loop(0, 4, rows, 0, unroll=4)

    loads[3].wait()
    loads[5].wait()
    for s in range(S):
        arrived(0, s)
        xs[s] = spectrum(0, s, SPEC)
        halves(xs[s])
        first, second = mix_rows(w32)
        back_to_rows(1, s, first - sgn * pltpu.roll(second, 64, 1), MODE)
        exchange(1, s)
        to_group(xs, xall, s, 0)

    def swap(o, carry):
        wt32[pl.ds(pl.multiple_of(o * 64, 64), 64), :] = w32[pl.ds(o, 64, stride=64), :]
        return carry

    lax.fori_loop(0, C, swap, 0)
    lga[...] = jnp.zeros_like(lga)

    my_plane = lax.div(me, 8)

    def to_plane(src_of, dst, n):
        for k in range(1, 8):
            other = lax.rem(me_y + k // 4, 2) * 4 + lax.rem(me_x + k % 4, 4)
            pltpu.make_async_remote_copy(
                src_ref=src_of(other), dst_ref=dst.at[my_plane], send_sem=lg_send.at[n], recv_sem=lg_recv.at[n],
                device_id={"tile": other * 8 + me_z}, device_id_type=MESH).start()
        pltpu.make_async_copy(src_of(my_plane), dst.at[my_plane], lg_recv.at[n]).start()

    def collected(ref, n):
        pltpu.make_async_copy(ref, ref, lg_recv.at[n]).wait()

    def point_hop(n):
        if n == 0:
            lgs[...] = lga[:64] + pltpu.roll(lga[64:], 64, 1)
            for j in range(1, N_DP):
                pltpu.make_async_remote_copy(
                    src_ref=lgs, dst_ref=lgd.at[my], send_sem=lg_send.at[0], recv_sem=lg_recv.at[0],
                    device_id={"dp": group(j)}, device_id_type=MESH).start()
            pltpu.make_async_copy(lgs, lgd.at[my], lg_recv.at[0]).start()
        elif n == 1:
            collected(lgd, 0)
            lgp[...] = jnp.sum(lgd[...], axis=0).reshape(8, 8, 128)
            to_plane(lambda other: lgp.at[other], lgr, 1)
        elif n == 2:
            collected(lgr, 1)
            lge[...] = jnp.sum(lgr[...], axis=0)
            for dz in range(1, 8):
                z = lax.rem(me_z + dz, 8)
                pltpu.make_async_remote_copy(
                    src_ref=lge, dst_ref=lgz.at[me_z], send_sem=lg_send.at[2], recv_sem=lg_recv.at[2],
                    device_id={"tile": me - me_z + z}, device_id_type=MESH).start()
            pltpu.make_async_copy(lge, lgz.at[me_z], lg_recv.at[2]).start()
        elif n == 3:
            collected(lgz, 2)
            lgq[...] = jnp.sum(lgz[...], axis=0)
            to_plane(lambda other: lgq, lgf, 3)
        else:
            collected(lgf, 3)
            lg[...] = lgf[...].reshape(C, 128)[:, :C]

    for s in range(S):
        arrived(1, s)
        b32[...] = rcv[1, s].astype(F32)

        def gate(r, carry):
            at = pl.ds(pl.multiple_of(r * 128, 128), 128)
            spectral = b32[pl.ds(r, 128, stride=RH), :].T.astype(BF16)
            tile = v[s, at, :]
            pre = mm(spectral, col[...]) + mm(mix[0].astype(BF16), tile)
            grad = (rows_of(ct.at[s], r) * gelu_slope(pre)).astype(BF16)
            gg[s, at, :] = grad
            m32[pl.ds(r, 128, stride=RH), :] = mm_nt(col[...], grad)
            lga[...] += mm_nt(tile, grad)
            return carry

        lax.fori_loop(0, RH, gate, 0, unroll=4)
        pack(2, s)
        if s == S - 1:
            point_hop(0)
        exchange(2, s)

    for s in range(S):
        arrived(2, s)
        ds[s] = spectrum(2, s, MODE)
        to_group(ds, dall, s, 1)
        halves(ds[s])
        first, second = mix_rows(wt32)
        back_to_rows(3, s, pltpu.roll(second, 64, 1) + sgn * first, SPEC)
        point_hop(1 + s)
        exchange(3, s)


    pltpu.make_async_copy(xall, xall, dp_recv.at[0]).wait()
    pltpu.make_async_copy(dall, dall, dp_recv.at[1]).wait()
    for g in range(N_DP):
        for s in range(S):
            n = g * S + s
            wide = xall[g, s].astype(F32)
            other = pltpu.roll(wide, 64, 1)
            x1[n] = jnp.where(low, wide, other)
            x2[n] = jnp.where(low, other, -wide)
            grad = dall[g, s].astype(F32)
            d1[n] = grad
            d2[n] = pltpu.roll(grad, 64, 1)

    def outer(c, carry):
        even = jnp.zeros((C, 128), F32)
        odd = jnp.zeros((C, 128), F32)
        for n in range(N_DP * S):
            first, second = d1[n], d2[n]
            even += x1[n, pl.ds(2 * c, 1), :] * first + x2[n, pl.ds(2 * c, 1), :] * second
            odd += x1[n, pl.ds(2 * c + 1, 1), :] * first + x2[n, pl.ds(2 * c + 1, 1), :] * second
        at = pl.multiple_of(c * 128, 128)
        mg[pl.ds(at, 64), :] = even
        mg[pl.ds(at + 64, 64), :] = odd
        return carry

    lax.fori_loop(0, C // 2, outer, 0)
    point_hop(3)

    mixl[...] = mix[1].astype(BF16)
    coll[...] = col[...]
    pointwise_part(gg.at[0], mixl, v32)
    pointwise_part(gg.at[1], mixl, wide1)
    arrived(3, 0)
    input_gradient(rcv.at[3, 0], v32, col, b32, t32, og, lambda n: None)

    point_hop(4)
    arrived(3, 1)
    last[...] = rcv[3, 1]

    for phase in range(4):
        for s in range(S):
            sent = snd.at[phase, s, pl.ds(0, 16 * (N_TILE - 1)), :]
            pltpu.make_async_copy(sent, sent, send_sem.at[phase, s]).wait()
    for n, ref in ((0, xall), (1, dall)):
        sent = ref.at[pl.ds(0, N_DP - 1)]
        pltpu.make_async_copy(sent, sent, dp_send.at[n]).wait()
    for n, ref, count in ((0, lgd, N_DP), (1, lgr, 8), (2, lgz, 8), (3, lgf, 8)):
        sent = ref.at[pl.ds(0, count - 1)]
        pltpu.make_async_copy(sent, sent, lg_send.at[n]).wait()


def step(inputs, cotangent, mode_weight, local_weight):
    rows = row_maps()
    col = jnp.asarray(column_rows(), BF16)
    inv = jnp.asarray(rows, BF16)
    fwd = jnp.asarray(np.ascontiguousarray(rows.T), BF16)
    dma = pltpu.SemaphoreType.DMA
    vm = pltpu.VMEM
    here = pl.BlockSpec(memory_space=pltpu.VMEM)
    anywhere = pl.BlockSpec(memory_space=pl.ANY)
    ready = pl.pallas_call(
        kernel,
        out_shape=(
            jax.ShapeDtypeStruct((C * TH, W), BF16),
            jax.ShapeDtypeStruct((C * C, 2 * M1), F32),
            jax.ShapeDtypeStruct((C, C), F32),
            jax.ShapeDtypeStruct((1024, 128), BF16),
            jax.ShapeDtypeStruct((2, TH * C, 128), F32),
            jax.ShapeDtypeStruct((128, W), BF16),
        ),
        in_specs=[anywhere] * 7,
        out_specs=(here,) * 6,
        scratch_shapes=[
            vm((S, TH * C, W), BF16), vm((S, TH * C, W), BF16), vm((2, TH * C, 128), F32),
            vm((S, TH * C, W), BF16), vm((S, 2, TH * C, 128), F32),
            vm((C * C, 128), BF16), vm((C * C, 128), F32), vm((C * C, 128), F32),
            vm((C, C), BF16), vm((2, 128, 128), F32), vm((128, W), BF16), vm((1024, 256), BF16), vm((256, 1024), BF16),
            vm((1024, 128), F32), vm((1024, 128), F32), vm((1024, 128), F32), vm((128, 128), BF16),
            vm((S, TH * C, W), BF16),
            vm((4, S, 1024, 128), BF16), vm((4, S, 1024, 128), BF16),
            vm((S, C, 128), BF16), vm((S, C, 128), BF16),
            vm((N_DP, S, C, 128), BF16), vm((N_DP, S, C, 128), BF16),
            vm((C, 128), F32), vm((C, 128), F32),
            vm((N_DP * S, C, 128), F32), vm((N_DP * S, C, 128), F32),
            vm((N_DP * S, C, 128), F32), vm((N_DP * S, C, 128), F32),
            vm((128, 128), F32), vm((C, 128), F32),
            vm((N_DP, C, 128), F32), vm((8, 8, 128), F32), vm((8, 8, 128), F32),
            vm((8, 128), F32), vm((8, 8, 128), F32), vm((8, 128), F32), vm((8, 8, 128), F32),
            dma((8,)), dma((4, S)), dma((4, S)), dma((2,)), dma((2,)), dma((4,)), dma((4,)),
        ],
        compiler_params=pltpu.CompilerParams(
            collective_id=0, has_side_effects=True, vmem_limit_bytes=40 << 20),
    )(*[pltpu.with_memory_space_constraint(a, pltpu.HBM) for a in (
        inputs.reshape(S, C * TH, W), cotangent.reshape(S, C * TH, W), mode_weight.reshape(C * C, 2 * M1),
        local_weight, col, inv, fwd)])
    og, mg, lg = pl.pallas_call(
        finish,
        out_shape=(
            jax.ShapeDtypeStruct((S, C * TH, W), BF16),
            jax.ShapeDtypeStruct((C * C, 2 * M1), F32),
            jax.ShapeDtypeStruct((C, C), F32),
        ),
        in_specs=[anywhere, anywhere, anywhere, here, here, here],
        out_specs=(anywhere,) * 3,
        scratch_shapes=[vm((1024, 128), F32), vm((1024, 128), F32), vm((C * TH, W), BF16), dma((7,))],
        compiler_params=pltpu.CompilerParams(vmem_limit_bytes=8 << 20),
    )(*ready)
    return og.reshape(S, C, TH, W), mg.reshape(1, C, C, 2 * M1), lg


def solution(mesh):
    in_specs = (P("dp", None, "tile", None), P("dp", None, "tile", None), P("tile", None, None, None), P())
    out_specs = (P("dp", None, "tile", None), P("tile", None, None, None), P())
    return jax.shard_map(step, mesh=mesh, in_specs=in_specs, out_specs=out_specs, check_vma=False)
```
